256 devices in a mesh: row: 32 (over x, z), feat: 8 (over y, core).
Axes of the slice: x: 4, y: 4, z: 8, core: 2. Of those that a mesh axis runs over, the one named last changes fastest.
Arguments:
- scores: float32 [192, 1024], P('row'), may hold values from -8 to 8, as said below
- labels: int32 [192, 1024], P('row'), may hold values from 0 to 4
- counts: int32 [192], P('row'), may hold values from 1 to 1024, 147456 in all
- bin_codes: int32 [192, 768, 1024], P('row', 'feat'), may hold values from 0 to 255
- row_child: int32 [192, 1024], P('row'), may hold values from 0 to 15
- smaller: int32 [8], replicated, may hold values from 0 to 1, as said below
- parent_hist: float32 [256, 8, 1536], P('row', None, 'feat'), may hold values from -10 to 10
Outputs:
- children: float32 [256, 8, 3072], P('row', None, 'feat')
- best_gain: float32 [8], replicated
The draws below stay inside these ranges and needn't reach their ends.
Inputs may be any that keep to these rules, and one draw needn't show every extreme that they name: Each query's scores never rise from one slot to the next. The counts of all queries sum to 147456, and some query is full. `smaller`: exactly half of the 8 parents have the value 1.
All inputs are finite; a program needn't handle non-finite values. No bound on the sum of `counts` on one device may be relied on, other than what follows from the above.
Results may differ from the reference program's by a relative error of at most 0.0028.
Values may be sent and summed in bfloat16 or wider, within the bound.
No kernel may reach another device: no remote copies, remote signals or barrier semaphores. Data moves between devices by JAX's collectives and lax.ppermute only.
A program may use at most 64 MiB of HBM per device.

```python
import math
import jax
import jax.numpy as jnp
import numpy as np
from jax import lax

F = 768
B = 256
Q = 1024
PARENTS = 8
QUERIES = 192


def draw_scores(key, part):
    raw_values = jnp.clip(2.0 * jax.random.normal(key, (QUERIES, Q), jnp.float32), -8.0, 8.0)
    return -jnp.sort(-raw_values, axis=1)


def draw_smaller(key, part):
    shuffled = jax.random.permutation(jax.random.fold_in(key, 17), jnp.arange(PARENTS, dtype=jnp.int32))
    return (shuffled % 2).astype(jnp.int32)


def plant(array, key, low, largest):
    place = [jax.random.randint(jax.random.fold_in(key, axis), (), 0, length) for axis, length in enumerate(array.shape)]
    widest = array.shape.index(max(array.shape))
    beside = place[:widest] + [(place[widest] + 1) % array.shape[widest]] + place[widest + 1:]
    return array.at[tuple(place)].set(low).at[tuple(beside)].set(largest)


def level_of(stream_key, extent, shards, least, high):
    level = 1.0
    for dim, blocks in shards:
        draws = jax.random.uniform(jax.random.fold_in(jax.random.fold_in(stream_key, 6), dim), (blocks,), jnp.float32, least / len(shards), high / len(shards))
        level = level * jnp.repeat(jnp.exp(draws), extent[dim] // blocks).reshape((-1,) + (1,) * (len(extent) - 1 - dim))
    return level


def cumulative_ranks(amount, slope):
    portions = [(1 << 20) // math.isqrt(standing ** slope) + 1 for standing in range(1, amount + 1)]
    scale = 1 + sum(portions) // (1 << 30)
    return np.cumsum(np.array([max(1, weight // scale) for weight in portions]))


def skewed_ids(stream_key, extent, number_of, skew):
    grid = cumulative_ranks(number_of, skew)
    ticket = jax.random.randint(jax.random.fold_in(stream_key, 1), extent, 0, int(grid[number_of - 1]))
    standing = jnp.searchsorted(jnp.asarray(grid, jnp.int32), ticket, side="right")
    return jax.random.permutation(jax.random.fold_in(stream_key, 2), number_of)[standing].astype(jnp.int32)


def length_profile(number_of, total, reach, slope):
    portions = [(1 << 20) // math.isqrt(rank ** slope) + 1 for rank in range(2, number_of + 1)]
    rest, holding = total - reach - (number_of - 1), [1] * (number_of - 1)
    while rest > 0:
        candidates = [i for i in range(number_of - 1) if holding[i] < reach]
        mass, budget = sum([portions[i] for i in candidates]), rest
        for i in candidates:
            more = min(reach - holding[i], max(1, budget * portions[i] // mass), rest)
            holding[i] = holding[i] + more
            rest = rest - more
    return np.array([reach] + holding)


def ragged_sizes(key, number_of, total, most, lean):
    if number_of == 2:
        one = jax.random.randint(key, (), max(1, total - most), min(most, total - 1) + 1)
        return jnp.stack([one, total - one])
    tallies = jnp.asarray(length_profile(number_of, total, most, lean), jnp.int32)
    couples = (number_of - 1) // 2
    source_of, sink = tallies[1:1 + 2 * couples:2], tallies[2:2 + 2 * couples:2]
    slack = jnp.minimum(source_of - 1, most - sink)
    passed = jax.random.randint(jax.random.fold_in(key, 1), (couples,), 0, 1 << 20) % (slack + 1)
    tallies = tallies.at[1:1 + 2 * couples:2].set(source_of - passed).at[2:2 + 2 * couples:2].set(sink + passed)
    return tallies[jax.random.permutation(jax.random.fold_in(key, 2), number_of)]


def bell_draw(own_key, extent, width, bound, pieces=(), held_as=jnp.bfloat16):
    loudness = level_of(own_key, extent, pieces, -0.22, 0.18) if pieces else 1.0
    drawn = jax.random.normal(own_key, extent, jnp.float32) * width * loudness
    return jnp.minimum(jnp.maximum(drawn, -bound), bound).astype(held_as)


def setup_inputs(seed: int = 0) -> dict:
    splits = jax.random.split(jax.random.key(seed), 8)
    scores = draw_scores(jax.random.fold_in(splits[7], 71), 0)
    labels = plant(skewed_ids(splits[1], (QUERIES, Q), 5, 2), jax.random.fold_in(splits[1], 3), 0, 4).astype(jnp.int32)
    counts = ragged_sizes(splits[2], QUERIES, QUERIES * Q * 3 // 4, Q, 2).astype(jnp.int32)
    bin_codes = plant(jax.random.randint(splits[3], (QUERIES, F, Q), 0, B), jax.random.fold_in(splits[3], 1), 0, B - 1).astype(jnp.int32)
    row_child = plant(jax.random.randint(splits[4], (QUERIES, Q), 0, 2 * PARENTS), jax.random.fold_in(splits[4], 1), 0, (2 * PARENTS) - 1).astype(jnp.int32)
    smaller = draw_smaller(jax.random.fold_in(splits[7], 71), 0)
    parent_hist = bell_draw(splits[6], (B, PARENTS, 2 * F), 2.0, 10.0, ((0, 32), (2, 8)), jnp.float32)
    return dict(scores=scores, labels=labels, counts=counts, bin_codes=bin_codes, row_child=row_child, smaller=smaller, parent_hist=parent_hist)


levels = 5
reg_lambda = 1.0


def query_terms(labels, counts):
    slot_count = labels.shape[1]
    position = jnp.arange(slot_count, dtype=jnp.int32)
    usable = position[None, :] < counts[:, None]
    grades = jnp.arange(levels, dtype=jnp.int32)
    same_grade = labels[:, :, None] == grades[None, None, :]
    label_hot = (same_grade & usable[:, :, None]).astype(jnp.int32)
    per_grade = jnp.sum(label_hot, axis=1)
    above_count = jnp.sum(per_grade[:, None, :] * (grades[None, None, :] > labels[:, :, None]).astype(jnp.int32), axis=2)
    running = jnp.cumsum(label_hot, axis=1) - label_hot
    before_count = jnp.sum(running * same_grade.astype(jnp.int32), axis=2)
    ideal_rank = above_count + before_count
    rel_gain = jnp.exp2(labels.astype(jnp.float32)) - 1.0
    discount = 1.0 / jnp.log2(position.astype(jnp.float32) + 2.0)
    ideal_terms = jnp.where(usable, rel_gain / jnp.log2(ideal_rank.astype(jnp.float32) + 2.0), 0.0)
    inv_ideal = 1.0 / jnp.maximum(jnp.sum(ideal_terms, axis=1), 1.0)
    return usable, rel_gain, discount, inv_ideal


def pair_block(row_scores, row_labels, row_gain, row_disc, row_usable, scores, labels, rel_gain, discount, usable, inv_ideal):
    score_gap = row_scores[:, :, None] - scores[:, None, :]
    higher = row_labels[:, :, None] > labels[:, None, :]
    live_pair = (row_labels[:, :, None] != labels[:, None, :]) & row_usable[:, :, None] & usable[:, None, :]
    pair_sign = jnp.where(higher, 1.0, -1.0)
    pair_prob = jax.nn.sigmoid(-pair_sign * score_gap)
    pair_weight = jnp.abs(row_gain[:, :, None] - rel_gain[:, None, :]) * jnp.abs(row_disc[None, :, None] - discount[None, None, :]) * inv_ideal[:, None, None]
    lam_grad = -jnp.sum(jnp.where(live_pair, pair_sign * pair_prob * pair_weight, 0.0), axis=2)
    lam_hess = jnp.sum(jnp.where(live_pair, pair_prob * (1.0 - pair_prob) * pair_weight, 0.0), axis=2)
    return lam_grad, lam_hess


def node_weights(lam_g16, lam_h16, row_child, smaller):
    parents = smaller.shape[0]
    built_node = 2 * jnp.arange(parents, dtype=jnp.int32) + smaller
    member = (row_child[:, :, None] == built_node[None, None, :]).astype(jnp.bfloat16)
    stats = jnp.stack((lam_g16, lam_h16), axis=-1)
    weights = member[:, :, :, None] * stats[:, :, None, :]
    return weights.reshape(row_child.shape[0], row_child.shape[1], parents * 2)


def split_gain(left_sums, totals):
    grad_left = left_sums[..., 0]
    hess_left = left_sums[..., 1]
    grad_total = totals[..., 0]
    hess_total = totals[..., 1]
    grad_right = grad_total - grad_left
    return (grad_left * grad_left / (hess_left + reg_lambda)
            + grad_right * grad_right / (hess_total - hess_left + reg_lambda)
            - grad_total * grad_total / (hess_total + reg_lambda))


def reference(scores, labels, counts, bin_codes, row_child, smaller, parent_hist):
    usable, rel_gain, discount, inv_ideal = query_terms(labels, counts)

    def per_query(packed):
        q_scores, q_labels, q_gain, q_usable, q_inv = packed
        lam_grad, lam_hess = pair_block(q_scores[None], q_labels[None], q_gain[None], discount, q_usable[None],
                                        q_scores[None], q_labels[None], q_gain[None], discount, q_usable[None], q_inv[None])
        return lam_grad[0], lam_hess[0]

    lam_grad, lam_hess = lax.map(per_query, (scores, labels, rel_gain, usable, inv_ideal))
    lam_g16 = lam_grad.astype(jnp.bfloat16)
    lam_h16 = lam_hess.astype(jnp.bfloat16)
    weights = node_weights(lam_g16, lam_h16, row_child, smaller)
    flat = weights.astype(jnp.float32).reshape(-1, 2 * PARENTS)

    def per_feature(index):
        code_rows = lax.dynamic_index_in_dim(bin_codes, index, 1, keepdims=False).reshape(-1)
        return jax.ops.segment_sum(flat, code_rows, num_segments=B)

    by_feature = lax.map(per_feature, jnp.arange(F, dtype=jnp.int32))
    built = jnp.transpose(by_feature.reshape(F, B, PARENTS, 2), (1, 2, 0, 3))
    sibling = parent_hist.reshape(B, PARENTS, F, 2) - built
    chosen = smaller[:, None] == jnp.arange(2, dtype=jnp.int32)[None, :]
    children = jnp.where(chosen[None, :, None, :, None], built[:, :, :, None, :], sibling[:, :, :, None, :])
    left_sums = jnp.cumsum(built, axis=0)
    totals = jnp.sum(built, axis=0)
    best_gain = jnp.max(split_gain(left_sums[:-1], totals[None]), axis=(0, 2))
    return children.reshape(B, PARENTS, 4 * F), best_gain
```

```python
import jax
import jax.numpy as jnp
from jax import lax
from jax.experimental import pallas as pl
from jax.experimental.pallas import tpu as pltpu
from jax.sharding import PartitionSpec as P

levels = 5
reg_lambda = 1.0
BI = 64
BJ = 256


def node_column(smaller_ref, parents):
    which = lax.broadcasted_iota(jnp.int32, (parents, 1), 0)
    column = jnp.zeros((parents, 1), jnp.int32)
    for p in range(parents):
        column = jnp.where(which == p, smaller_ref[p], column)
    return column


def lambda_kernel(
    counts_ref, smaller_ref, scores_ref, labels_ref, child_ref, weight_ref,
    exp_row, gain_row, disc_row, exp_col, gain_col, disc_col, row_grad, row_hess, col_grad, col_hess,
):
    query_dev, slots = scores_ref.shape
    parents = smaller_ref.shape[0]
    position = lax.broadcasted_iota(jnp.int32, (1, slots), 1)
    discount = 1.0 / jnp.log2(position.astype(jnp.float32) + 2.0)
    exp_row[...] = jnp.zeros_like(exp_row)
    gain_row[...] = jnp.zeros_like(gain_row)
    exp_row[0:query_dev, :] = jnp.exp(scores_ref[...])
    gain_row[0:query_dev, :] = jnp.exp2(labels_ref[...].astype(jnp.float32)) - 1.0
    exp_col[...] = exp_row[...].T
    gain_col[...] = gain_row[...].T
    disc_col[...] = jnp.broadcast_to(discount, (8, slots)).T
    row_grad[...] = jnp.zeros_like(row_grad)
    row_hess[...] = jnp.zeros_like(row_hess)
    col_grad[...] = jnp.zeros_like(col_grad)
    col_hess[...] = jnp.zeros_like(col_hess)
    for q in range(query_dev):
        disc_row[q : q + 1, :] = jnp.where(position < counts_ref[q], discount, 4.0)

    for q in range(query_dev):
        count = counts_ref[q]

        def row_block(ib, carry, q=q, count=count):
            first = pl.multiple_of(ib * BI, BI)
            e_i = jnp.broadcast_to(exp_col[pl.ds(first, BI), q : q + 1], (BI, BJ))
            g_i = jnp.broadcast_to(gain_col[pl.ds(first, BI), q : q + 1], (BI, BJ))
            d_i = jnp.broadcast_to(disc_col[pl.ds(first, BI), 0:1], (BI, BJ))

            def pair_tile(jb, sums):
                grad_sum, hess_sum = sums
                at = pl.multiple_of(jb * BJ, BJ)
                e_j = exp_row[q : q + 1, pl.ds(at, BJ)]
                g_j = gain_row[q : q + 1, pl.ds(at, BJ)]
                d_j = disc_row[q : q + 1, pl.ds(at, BJ)]
                inverse = 1.0 / (e_i + e_j)
                gain_gap = g_i - g_j
                disc_gap = jnp.maximum(d_i - d_j, 0.0)
                higher = gain_gap > 0.0
                part = gain_gap * disc_gap * inverse
                grad = part * jnp.where(higher, e_j, e_i)
                hess = jnp.abs(grad) * (inverse * jnp.where(higher, e_i, e_j))
                col_grad[q, :, pl.ds(at, BJ)] += jnp.sum(grad.reshape(BI // 8, 8, BJ), axis=0)
                col_hess[q, :, pl.ds(at, BJ)] += jnp.sum(hess.reshape(BI // 8, 8, BJ), axis=0)
                for k in range(0, BJ, 128):
                    grad_sum = grad_sum + grad[:, k : k + 128]
                    hess_sum = hess_sum + hess[:, k : k + 128]
                return grad_sum, hess_sum

            zero = jnp.zeros((BI, 128), jnp.float32)
            grad_sum, hess_sum = lax.fori_loop(
                (ib * BI) // BJ, (count + BJ - 1) // BJ, pair_tile, (zero, zero)
            )
            row_grad[pl.ds(first, BI), q : q + 1] = jnp.sum(grad_sum, axis=1, keepdims=True)
            row_hess[pl.ds(first, BI), q : q + 1] = jnp.sum(hess_sum, axis=1, keepdims=True)
            return carry

        lax.fori_loop(0, (count + BI - 1) // BI, row_block, 0)

    row_grad_t = row_grad[...].T
    row_hess_t = row_hess[...].T
    nodes = 2 * lax.broadcasted_iota(jnp.int32, (parents, 1), 0) + node_column(smaller_ref, parents)
    for q in range(query_dev):
        grade = labels_ref[q : q + 1, :]
        usable = position < counts_ref[q]
        ideal = jnp.zeros((1, slots), jnp.float32)
        ahead = jnp.zeros((1, 1), jnp.int32)
        for c in range(levels - 1, 0, -1):
            here = jnp.sum(((grade == c) & usable).astype(jnp.int32), axis=1, keepdims=True)
            span = (position >= ahead) & (position < ahead + here)
            ideal = ideal + jnp.where(span, float(2**c - 1), 0.0)
            ahead = ahead + here
        inv_ideal = 1.0 / jnp.maximum(jnp.sum(ideal * discount, axis=1, keepdims=True), 1.0)
        grad = (jnp.sum(col_grad[q], axis=0, keepdims=True) - row_grad_t[q : q + 1, :]) * inv_ideal
        hess = (jnp.sum(col_hess[q], axis=0, keepdims=True) + row_hess_t[q : q + 1, :]) * inv_ideal
        member = child_ref[q : q + 1, :] == nodes
        both = jnp.concatenate((jnp.where(member, grad, 0.0), jnp.where(member, hess, 0.0)), axis=0)
        weight_ref[:, q * slots : (q + 1) * slots] = both.astype(jnp.bfloat16)


def lambda_weights(scores, labels, counts, row_child, smaller):
    query_dev, slots = scores.shape
    parents = smaller.shape[0]
    vmem = pl.BlockSpec(memory_space=pltpu.VMEM)
    smem = pl.BlockSpec(memory_space=pltpu.SMEM)
    row = pltpu.VMEM((8, slots), jnp.float32)
    col = pltpu.VMEM((slots, 8), jnp.float32)
    acc = pltpu.VMEM((query_dev, 8, slots), jnp.float32)
    return pl.pallas_call(
        lambda_kernel,
        out_shape=jax.ShapeDtypeStruct((2 * parents, query_dev * slots), jnp.bfloat16),
        in_specs=[smem, smem, vmem, vmem, vmem],
        out_specs=vmem,
        scratch_shapes=[row, row, row, col, col, col, col, col, acc, acc],
        name="lambda_weights",
    )(counts, smaller, scores, labels, row_child)


def histogram_kernel(codes_ref, weight_ref, hist_ref):
    query_dev, feats, slots = codes_ref.shape
    one = jnp.ones((), jnp.bfloat16)
    zero = jnp.zeros((), jnp.bfloat16)
    low_mark = lax.broadcasted_iota(jnp.int32, (64, 1), 0).astype(jnp.float32).astype(jnp.bfloat16)
    for group in range(feats // 4):
        total = jnp.zeros((256, 256), jnp.float32)
        for q in range(query_dev):
            weight = weight_ref[:, q * slots : (q + 1) * slots]
            lhs = []
            rhs = []
            for f in range(4 * group, 4 * group + 4):
                code = codes_ref[q, f : f + 1, :]
                high = jnp.broadcast_to((code >> 6).astype(jnp.float32), (16, slots)).astype(jnp.bfloat16)
                low = jnp.broadcast_to((code & 63).astype(jnp.float32), (64, slots)).astype(jnp.bfloat16)
                for h in range(4):
                    lhs.append(jnp.where(high == jnp.asarray(h, jnp.bfloat16), weight, zero))
                rhs.append(jnp.where(low == low_mark, one, zero))
            total += lax.dot_general(
                jnp.concatenate(lhs, axis=0), jnp.concatenate(rhs, axis=0),
                (((1,), (1,)), ((), ())), preferred_element_type=jnp.float32,
            )
        for k in range(4):
            pieces = [total[k * 64 + h * 16 : k * 64 + h * 16 + 16, k * 64 : k * 64 + 64] for h in range(4)]
            hist_ref[4 * group + k] = jnp.concatenate(pieces, axis=1).astype(jnp.bfloat16)


def histograms(bin_codes, weight):
    query_dev, feat_dev, slots = bin_codes.shape
    return pl.pallas_call(
        histogram_kernel,
        grid=(feat_dev // 8,),
        out_shape=jax.ShapeDtypeStruct((feat_dev, 16, 256), jnp.bfloat16),
        in_specs=[
            pl.BlockSpec((query_dev, 8, slots), lambda i: (0, i, 0)),
            pl.BlockSpec(weight.shape, lambda i: (0, 0)),
        ],
        out_specs=pl.BlockSpec((8, 16, 256), lambda i: (i, 0, 0)),
        name="histograms",
    )(bin_codes, weight)


def gain_kernel(parts_ref, send_ref):
    sources, rows, bins = parts_ref.shape
    built = jnp.sum(parts_ref[...].astype(jnp.float32), axis=0)
    below = lax.broadcasted_iota(jnp.int32, (bins, bins), 0)
    upto = lax.broadcasted_iota(jnp.int32, (bins, bins), 1)
    left = jnp.dot(
        built, (below <= upto).astype(jnp.float32),
        precision=lax.Precision.HIGHEST, preferred_element_type=jnp.float32,
    )
    threshold = lax.broadcasted_iota(jnp.int32, (8, bins), 1)
    best = jnp.full((8, 1), -jnp.inf, jnp.float32)
    for f in range(rows // 16):
        grad_left = left[f * 16 : f * 16 + 8]
        hess_left = left[f * 16 + 8 : f * 16 + 16]
        grad_total = grad_left[:, bins - 1 : bins]
        hess_total = hess_left[:, bins - 1 : bins]
        grad_right = grad_total - grad_left
        gain = (
            grad_left * grad_left / (hess_left + reg_lambda)
            + grad_right * grad_right / (hess_total - hess_left + reg_lambda)
            - grad_total * grad_total / (hess_total + reg_lambda)
        )
        gain = jnp.where(threshold < bins - 1, gain, -jnp.inf)
        best = jnp.maximum(best, jnp.max(gain, axis=1, keepdims=True))
    stacked = jnp.concatenate(
        (built, jnp.broadcast_to(best, (8, bins)), jnp.zeros((128 - rows - 8, bins), jnp.float32)), axis=0
    )
    send_ref[...] = stacked.T.reshape(send_ref.shape)


def children_kernel(smaller_ref, parts_ref, parent_ref, children_ref, best_ref):
    sources, bin_span, lanes = parts_ref.shape
    parents, width = children_ref.shape[1:]
    group = width // sources
    column = lax.broadcasted_iota(jnp.int32, (sources, width), 1)
    source = lax.broadcasted_iota(jnp.int32, (sources, width), 0)
    spread = (column // group == source).astype(jnp.float32)
    rows = group * parents // 2
    row = lax.broadcasted_iota(jnp.int32, (rows, width), 0)
    col = lax.broadcasted_iota(jnp.int32, (rows, width), 1)
    match = (row // (2 * parents) == (col % group) // 4) & ((row // parents) % 2 == col % 2)
    pick_row = lax.broadcasted_iota(jnp.int32, (width // 2, width), 0)
    pick_col = lax.broadcasted_iota(jnp.int32, (width // 2, width), 1)
    pick = (pick_row == (pick_col // 4) * 2 + pick_col % 2).astype(jnp.float32)
    side = (lax.broadcasted_iota(jnp.int32, (parents, width), 1) // 2) % 2
    chosen = side == node_column(smaller_ref, parents)
    parent = jnp.dot(
        parent_ref[...].reshape(bin_span * parents, width // 2), pick,
        precision=lax.Precision.HIGHEST, preferred_element_type=jnp.float32,
    )
    for b in range(bin_span):
        wide = lax.dot_general(
            parts_ref[:, b, :], spread, (((0,), (0,)), ((), ())),
            precision=lax.Precision.HIGHEST, preferred_element_type=jnp.float32,
        )
        kept = jnp.where(match, wide[:rows], 0.0)
        built = jnp.sum(kept.reshape(rows // parents, parents, width), axis=0)
        children_ref[b] = jnp.where(chosen, built, parent[b * parents : (b + 1) * parents] - built)
    best = jnp.max(parts_ref[:, 0, :], axis=0, keepdims=True)
    best_ref[...] = jnp.broadcast_to(best[None], best_ref.shape)


def shards(scores, labels, counts, bin_codes, row_child, smaller, parent_hist):
    feat_dev = bin_codes.shape[1]
    bin_span, parents, _ = parent_hist.shape
    row_count = lax.axis_size("row")
    feat_count = lax.axis_size("feat")
    rows = feat_dev // row_count * 2 * parents
    bins = bin_span * row_count
    weight = lambda_weights(scores, labels, counts, row_child, smaller)
    hist = histograms(bin_codes, weight)
    parts = lax.all_to_all(hist.reshape(row_count, rows, bins), "row", 0, 0, tiled=True)
    vmem = pl.BlockSpec(memory_space=pltpu.VMEM)
    smem = pl.BlockSpec(memory_space=pltpu.SMEM)
    send = pl.pallas_call(
        gain_kernel,
        out_shape=jax.ShapeDtypeStruct((row_count, bin_span, 128), jnp.float32),
        in_specs=[vmem], out_specs=vmem, name="gains",
    )(parts)
    own = lax.all_to_all(send, "row", 0, 0, tiled=True)
    children, best = pl.pallas_call(
        children_kernel,
        out_shape=(
            jax.ShapeDtypeStruct((bin_span, parents, feat_dev * 4), jnp.float32),
            jax.ShapeDtypeStruct((feat_count, 8, 128), jnp.float32),
        ),
        in_specs=[smem, vmem, vmem], out_specs=(vmem, vmem), name="children",
    )(smaller, own, parent_hist)
    best = jnp.max(lax.all_to_all(best, "feat", 0, 0, tiled=True), axis=0)
    return children, best[0, rows : rows + parents]


def solution(mesh):
    placed = (
        P("row", None), P("row", None), P("row"), P("row", "feat", None),
        P("row", None), P(), P("row", None, "feat"),
    )
    return jax.shard_map(
        shards, mesh=mesh, in_specs=placed, out_specs=(P("row", None, "feat"), P()), check_vma=False
    )
```

```python
import jax
import jax.numpy as jnp
from jax import lax
from jax.experimental import pallas as pl
from jax.experimental.pallas import tpu as pltpu
from jax.sharding import PartitionSpec as P

levels = 5
reg_lambda = 1.0
SHARE = 128
EARLY = 2


def node_column(smaller_ref, parents):
    which = lax.broadcasted_iota(jnp.int32, (parents, 1), 0)
    column = jnp.zeros((parents, 1), jnp.int32)
    for p in range(parents):
        column = jnp.where(which == p, smaller_ref[p], column)
    return column


def lambda_kernel(
    counts_ref, scores_ref, labels_ref, lam_ref,
    exp_row, gain_row, disc_row, exp_col, gain_col, disc_col, lam_rows,
):
    query_dev, slots = scores_ref.shape
    own = pl.multiple_of(lax.axis_index("feat") * SHARE, SHARE)
    position = lax.broadcasted_iota(jnp.int32, (1, slots), 1)
    discount = 1.0 / jnp.log2(position.astype(jnp.float32) + 2.0)
    disc_row[...] = jnp.broadcast_to(discount, (8, slots))
    exp_row[...] = jnp.zeros_like(exp_row)
    gain_row[...] = jnp.zeros_like(gain_row)
    lam_rows[...] = jnp.zeros_like(lam_rows)
    score_exp = jnp.exp(scores_ref[...])
    rel_gain = jnp.exp2(labels_ref[...].astype(jnp.float32)) - 1.0
    for q in range(query_dev):
        usable = position < counts_ref[q]
        exp_row[q : q + 1, :] = jnp.where(usable, score_exp[q : q + 1], 0.0)
        gain_row[q : q + 1, :] = jnp.where(usable, rel_gain[q : q + 1], -1.0)
    exp_col[...] = exp_row[...].T
    gain_col[...] = gain_row[...].T
    disc_col[...] = disc_row[...].T

    for q in range(query_dev):
        count = counts_ref[q]
        e_i = exp_row[q : q + 1, pl.ds(own, SHARE)]
        g_i = gain_row[q : q + 1, pl.ds(own, SHARE)]
        d_i = disc_row[0:1, pl.ds(own, SHARE)]

        def partners(jb, sums, q=q, e_i=e_i, g_i=g_i, d_i=d_i):
            grad_sum, hess_sum = sums
            at = pl.multiple_of(jb * 128, 128)
            e_j = exp_col[pl.ds(at, 128), q : q + 1]
            g_j = gain_col[pl.ds(at, 128), q : q + 1]
            d_j = disc_col[pl.ds(at, 128), 0:1]
            inverse = 1.0 / (e_i + e_j)
            gain_gap = g_i - g_j
            higher = gain_gap > 0.0
            part = gain_gap * (jnp.abs(d_i - d_j) * inverse)
            grad = part * jnp.where(higher, e_j, e_i)
            hess = jnp.abs(grad) * (inverse * jnp.where(higher, e_i, e_j))
            grad_sum = grad_sum + jnp.sum(grad.reshape(16, 8, SHARE), axis=0)
            hess_sum = hess_sum + jnp.sum(hess.reshape(16, 8, SHARE), axis=0)
            return grad_sum, hess_sum

        zero = jnp.zeros((8, SHARE), jnp.float32)
        last = jnp.where(own < count, (count + 127) // 128, 0)
        grad_sum, hess_sum = lax.fori_loop(0, last, partners, (zero, zero))

        grade = labels_ref[q : q + 1, :]
        usable = position < count
        ideal = jnp.zeros((1, slots), jnp.float32)
        ahead = jnp.zeros((1, 1), jnp.int32)
        for c in range(levels - 1, 0, -1):
            here = jnp.sum(((grade == c) & usable).astype(jnp.int32), axis=1, keepdims=True)
            span = (position >= ahead) & (position < ahead + here)
            ideal = ideal + jnp.where(span, float(2**c - 1), 0.0)
            ahead = ahead + here
        inv_ideal = 1.0 / jnp.maximum(jnp.sum(ideal * discount, axis=1, keepdims=True), 1.0)
        mine = own + lax.broadcasted_iota(jnp.int32, (1, SHARE), 1) < count
        grad = -jnp.sum(grad_sum, axis=0, keepdims=True) * inv_ideal
        hess = jnp.sum(hess_sum, axis=0, keepdims=True) * inv_ideal
        lam_rows[q : q + 1, :] = jnp.where(mine, grad, 0.0)
        lam_rows[8 + q : 9 + q, :] = jnp.where(mine, hess, 0.0)

    lam_ref[...] = jnp.broadcast_to(lam_rows[...].astype(jnp.bfloat16)[None], lam_ref.shape)


def lambdas(scores, labels, counts):
    query_dev, slots = scores.shape
    vmem = pl.BlockSpec(memory_space=pltpu.VMEM)
    smem = pl.BlockSpec(memory_space=pltpu.SMEM)
    row = pltpu.VMEM((8, slots), jnp.float32)
    col = pltpu.VMEM((slots, 8), jnp.float32)
    return pl.pallas_call(
        lambda_kernel,
        out_shape=jax.ShapeDtypeStruct((slots // SHARE, 16, SHARE), jnp.bfloat16),
        in_specs=[smem, vmem, vmem],
        out_specs=vmem,
        scratch_shapes=[row, row, row, col, col, col, pltpu.VMEM((16, SHARE), jnp.float32)],
        name="lambdas",
    )(counts, scores, labels)


def weight_kernel(smaller_ref, lam_ref, child_ref, weight_ref):
    query_dev, slots = child_ref.shape
    parents = smaller_ref.shape[0]
    nodes = 2 * lax.broadcasted_iota(jnp.int32, (parents, 1), 0) + node_column(smaller_ref, parents)
    lam = jnp.concatenate([lam_ref[k].astype(jnp.float32) for k in range(lam_ref.shape[0])], axis=1)
    for q in range(query_dev):
        member = child_ref[q : q + 1, :] == nodes
        grad = jnp.where(member, lam[q : q + 1], 0.0)
        hess = jnp.where(member, lam[8 + q : 9 + q], 0.0)
        weight_ref[:, q * slots : (q + 1) * slots] = jnp.concatenate((grad, hess), axis=0).astype(jnp.bfloat16)


def histogram_kernel(codes_ref, weight_ref, after_ref, hist_ref):
    del after_ref
    query_dev, feats, slots = codes_ref.shape
    one = jnp.ones((), jnp.bfloat16)
    zero = jnp.zeros((), jnp.bfloat16)
    low_mark = lax.broadcasted_iota(jnp.int32, (64, 1), 0).astype(jnp.float32).astype(jnp.bfloat16)
    for group in range(feats // 4):
        total = jnp.zeros((256, 256), jnp.float32)
        for q in range(query_dev):
            weight = weight_ref[:, q * slots : (q + 1) * slots]
            lhs = []
            rhs = []
            for f in range(4 * group, 4 * group + 4):
                code = codes_ref[q, f : f + 1, :]
                high = jnp.broadcast_to((code >> 6).astype(jnp.float32), (16, slots)).astype(jnp.bfloat16)
                low = jnp.broadcast_to((code & 63).astype(jnp.float32), (64, slots)).astype(jnp.bfloat16)
                for h in range(4):
                    lhs.append(jnp.where(high == jnp.asarray(h, jnp.bfloat16), weight, zero))
                rhs.append(jnp.where(low == low_mark, one, zero))
            total += lax.dot_general(
                jnp.concatenate(lhs, axis=0), jnp.concatenate(rhs, axis=0),
                (((1,), (1,)), ((), ())), preferred_element_type=jnp.float32,
            )
        for k in range(4):
            pieces = [total[k * 64 + h * 16 : k * 64 + h * 16 + 16, k * 64 : k * 64 + 64] for h in range(4)]
            hist_ref[4 * group + k] = jnp.concatenate(pieces, axis=1).astype(jnp.bfloat16)


def histograms(bin_codes, weight, after, first, count):
    query_dev, feat_dev, slots = bin_codes.shape
    return pl.pallas_call(
        histogram_kernel,
        grid=(count // 8,),
        out_shape=jax.ShapeDtypeStruct((count, 16, 256), jnp.bfloat16),
        in_specs=[
            pl.BlockSpec((query_dev, 8, slots), lambda i: (0, i + first // 8, 0)),
            pl.BlockSpec(weight.shape, lambda i: (0, 0)),
            pl.BlockSpec(memory_space=pl.ANY),
        ],
        out_specs=pl.BlockSpec((8, 16, 256), lambda i: (i, 0, 0)),
        name="histograms",
    )(bin_codes, weight, after)


def gain_kernel(early_ref, late_ref, send_ref):
    rows = early_ref.shape[1] + late_ref.shape[1]
    bins = early_ref.shape[2]
    built = jnp.concatenate(
        (
            jnp.sum(early_ref[...].astype(jnp.float32), axis=0),
            jnp.sum(late_ref[...].astype(jnp.float32), axis=0),
        ),
        axis=0,
    )
    below = lax.broadcasted_iota(jnp.int32, (bins, bins), 0)
    upto = lax.broadcasted_iota(jnp.int32, (bins, bins), 1)
    left = jnp.dot(
        built, (below <= upto).astype(jnp.float32),
        precision=lax.Precision.HIGHEST, preferred_element_type=jnp.float32,
    )
    threshold = lax.broadcasted_iota(jnp.int32, (8, bins), 1)
    best = jnp.full((8, 1), -jnp.inf, jnp.float32)
    for f in range(rows // 16):
        grad_left = left[f * 16 : f * 16 + 8]
        hess_left = left[f * 16 + 8 : f * 16 + 16]
        grad_total = grad_left[:, bins - 1 : bins]
        hess_total = hess_left[:, bins - 1 : bins]
        grad_right = grad_total - grad_left
        gain = (
            grad_left * grad_left / (hess_left + reg_lambda)
            + grad_right * grad_right / (hess_total - hess_left + reg_lambda)
            - grad_total * grad_total / (hess_total + reg_lambda)
        )
        gain = jnp.where(threshold < bins - 1, gain, -jnp.inf)
        best = jnp.maximum(best, jnp.max(gain, axis=1, keepdims=True))
    stacked = jnp.concatenate(
        (built, jnp.broadcast_to(best, (8, bins)), jnp.zeros((128 - rows - 8, bins), jnp.float32)), axis=0
    )
    send_ref[...] = stacked.T.reshape(send_ref.shape)


def children_kernel(smaller_ref, parts_ref, parent_ref, children_ref):
    sources, bin_span, lanes = parts_ref.shape
    parents, width = children_ref.shape[1:]
    group = width // sources
    early = EARLY * sources

    def place(column):
        feat = column // 4
        is_early = feat < early
        owner = jnp.where(is_early, feat // EARLY, (feat - early) % sources)
        local = jnp.where(is_early, feat % EARLY, EARLY + (feat - early) // sources)
        return owner, local

    column = lax.broadcasted_iota(jnp.int32, (sources, width), 1)
    source = lax.broadcasted_iota(jnp.int32, (sources, width), 0)
    spread = (place(column)[0] == source).astype(jnp.float32)
    rows = group * parents // 2
    row = lax.broadcasted_iota(jnp.int32, (rows, width), 0)
    col = lax.broadcasted_iota(jnp.int32, (rows, width), 1)
    match = (row // (2 * parents) == place(col)[1]) & ((row // parents) % 2 == col % 2)
    pick_row = lax.broadcasted_iota(jnp.int32, (width // 2, width), 0)
    pick_col = lax.broadcasted_iota(jnp.int32, (width // 2, width), 1)
    pick = (pick_row == (pick_col // 4) * 2 + pick_col % 2).astype(jnp.float32)
    side = (lax.broadcasted_iota(jnp.int32, (parents, width), 1) // 2) % 2
    chosen = side == node_column(smaller_ref, parents)
    parent = jnp.dot(
        parent_ref[...].reshape(bin_span * parents, width // 2), pick,
        precision=lax.Precision.HIGHEST, preferred_element_type=jnp.float32,
    )
    for b in range(bin_span):
        wide = lax.dot_general(
            parts_ref[:, b, :], spread, (((0,), (0,)), ((), ())),
            precision=lax.Precision.HIGHEST, preferred_element_type=jnp.float32,
        )
        kept = jnp.where(match, wide[:rows], 0.0)
        built = jnp.sum(kept.reshape(rows // parents, parents, width), axis=0)
        children_ref[b] = jnp.where(chosen, built, parent[b * parents : (b + 1) * parents] - built)


def shards(scores, labels, counts, bin_codes, row_child, smaller, parent_hist):
    feat_dev = bin_codes.shape[1]
    bin_span, parents, _ = parent_hist.shape
    row_count = lax.axis_size("row")
    feat_count = lax.axis_size("feat")
    rows = feat_dev // row_count * 2 * parents
    bins = bin_span * row_count
    vmem = pl.BlockSpec(memory_space=pltpu.VMEM)
    smem = pl.BlockSpec(memory_space=pltpu.SMEM)
    lam = lax.all_to_all(lambdas(scores, labels, counts), "feat", 0, 0, tiled=True)
    weight = pl.pallas_call(
        weight_kernel,
        out_shape=jax.ShapeDtypeStruct((2 * parents, row_child.size), jnp.bfloat16),
        in_specs=[smem, vmem, vmem], out_specs=vmem, name="weights",
    )(smaller, lam, row_child)
    received = []
    first, hist = 0, weight
    for count in (EARLY * row_count, feat_dev - EARLY * row_count):
        hist = histograms(bin_codes, weight, hist, first, count)
        parts = hist.reshape(row_count, count // row_count * 2 * parents, bins)
        received.append(lax.all_to_all(parts, "row", 0, 0, tiled=True))
        first += count
    send = pl.pallas_call(
        gain_kernel,
        out_shape=jax.ShapeDtypeStruct((row_count, bin_span, 128), jnp.float32),
        in_specs=[vmem, vmem], out_specs=vmem, name="gains",
    )(*received)
    own = lax.all_to_all(send, "row", 0, 0, tiled=True)
    best = jnp.broadcast_to(jnp.max(own, axis=0)[None], (feat_count, bin_span, 128))
    best = jnp.max(lax.all_to_all(best, "feat", 0, 0, tiled=True), axis=0)
    children = pl.pallas_call(
        children_kernel,
        out_shape=jax.ShapeDtypeStruct((bin_span, parents, feat_dev * 4), jnp.float32),
        in_specs=[smem, vmem, vmem], out_specs=vmem, name="children",
    )(smaller, own, parent_hist)
    return children, best[0, rows : rows + parents]


def solution(mesh):
    placed = (
        P("row", None), P("row", None), P("row"), P("row", "feat", None),
        P("row", None), P(), P("row", None, "feat"),
    )
    return jax.shard_map(
        shards, mesh=mesh, in_specs=placed, out_specs=(P("row", None, "feat"), P()), check_vma=False
    )
```

```python
import jax
import jax.numpy as jnp
from jax import lax
from jax.experimental import pallas as pl
from jax.experimental.pallas import tpu as pltpu
from jax.sharding import PartitionSpec as P

levels = 5
reg_lambda = 1.0
SHARE = 128
HIGHS = 4
LOWS = 256 // HIGHS
CHUNK = 512
BLOCK = 256
FEATS = 96


def node_column(smaller_ref, parents):
    which = lax.broadcasted_iota(jnp.int32, (parents, 1), 0)
    column = jnp.zeros((parents, 1), jnp.int32)
    for p in range(parents):
        column = jnp.where(which == p, smaller_ref[p], column)
    return column


def lambda_kernel(
    counts_ref, scores_ref, labels_ref, lam_ref,
    exp_row, gain_row, disc_row, exp_col, gain_col, disc_col, lam_rows,
):
    query_dev, slots = scores_ref.shape
    own = pl.multiple_of(lax.axis_index("feat") * SHARE, SHARE)
    position = lax.broadcasted_iota(jnp.int32, (1, slots), 1)
    discount = 1.0 / jnp.log2(position.astype(jnp.float32) + 2.0)
    disc_row[...] = jnp.broadcast_to(discount, (8, slots))
    exp_row[...] = jnp.zeros_like(exp_row)
    gain_row[...] = jnp.zeros_like(gain_row)
    lam_rows[...] = jnp.zeros_like(lam_rows)
    score_exp = jnp.exp(scores_ref[...])
    rel_gain = jnp.exp2(labels_ref[...].astype(jnp.float32)) - 1.0
    for q in range(query_dev):
        usable = position < counts_ref[q]
        exp_row[q : q + 1, :] = jnp.where(usable, score_exp[q : q + 1], 0.0)
        gain_row[q : q + 1, :] = jnp.where(usable, rel_gain[q : q + 1], -1.0)
    exp_col[...] = exp_row[...].T
    gain_col[...] = gain_row[...].T
    disc_col[...] = disc_row[...].T

    for q in range(query_dev):
        count = counts_ref[q]
        e_i = exp_row[q : q + 1, pl.ds(own, SHARE)]
        g_i = gain_row[q : q + 1, pl.ds(own, SHARE)]
        d_i = disc_row[0:1, pl.ds(own, SHARE)]

        def partners(jb, sums, q=q, e_i=e_i, g_i=g_i, d_i=d_i):
            grad_sum, hess_sum = sums
            at = pl.multiple_of(jb * 128, 128)
            e_j = exp_col[pl.ds(at, 128), q : q + 1]
            g_j = gain_col[pl.ds(at, 128), q : q + 1]
            d_j = disc_col[pl.ds(at, 128), 0:1]
            inverse = 1.0 / (e_i + e_j)
            gain_gap = g_i - g_j
            higher = gain_gap > 0.0
            part = gain_gap * (jnp.abs(d_i - d_j) * inverse)
            grad = part * jnp.where(higher, e_j, e_i)
            hess = jnp.abs(grad) * (inverse * jnp.where(higher, e_i, e_j))
            grad_sum = grad_sum + jnp.sum(grad.reshape(16, 8, SHARE), axis=0)
            hess_sum = hess_sum + jnp.sum(hess.reshape(16, 8, SHARE), axis=0)
            return grad_sum, hess_sum

        zero = jnp.zeros((8, SHARE), jnp.float32)
        last = jnp.where(own < count, (count + 127) // 128, 0)
        grad_sum, hess_sum = lax.fori_loop(0, last, partners, (zero, zero))

        grade = labels_ref[q : q + 1, :]
        usable = position < count
        ideal = jnp.zeros((1, slots), jnp.float32)
        ahead = jnp.zeros((1, 1), jnp.int32)
        for c in range(levels - 1, 0, -1):
            here = jnp.sum(((grade == c) & usable).astype(jnp.int32), axis=1, keepdims=True)
            span = (position >= ahead) & (position < ahead + here)
            ideal = ideal + jnp.where(span, float(2**c - 1), 0.0)
            ahead = ahead + here
        inv_ideal = 1.0 / jnp.maximum(jnp.sum(ideal * discount, axis=1, keepdims=True), 1.0)
        mine = own + lax.broadcasted_iota(jnp.int32, (1, SHARE), 1) < count
        grad = -jnp.sum(grad_sum, axis=0, keepdims=True) * inv_ideal
        hess = jnp.sum(hess_sum, axis=0, keepdims=True) * inv_ideal
        lam_rows[q : q + 1, :] = jnp.where(mine, grad, 0.0)
        lam_rows[8 + q : 9 + q, :] = jnp.where(mine, hess, 0.0)

    lam_ref[...] = jnp.broadcast_to(lam_rows[...].astype(jnp.bfloat16)[None], lam_ref.shape)


def lambdas(scores, labels, counts):
    query_dev, slots = scores.shape
    vmem = pl.BlockSpec(memory_space=pltpu.VMEM)
    smem = pl.BlockSpec(memory_space=pltpu.SMEM)
    row = pltpu.VMEM((8, slots), jnp.float32)
    col = pltpu.VMEM((slots, 8), jnp.float32)
    return pl.pallas_call(
        lambda_kernel,
        out_shape=jax.ShapeDtypeStruct((slots // SHARE, 16, SHARE), jnp.bfloat16),
        in_specs=[smem, vmem, vmem],
        out_specs=vmem,
        scratch_shapes=[row, row, row, col, col, col, pltpu.VMEM((16, SHARE), jnp.float32)],
        name="lambdas",
    )(counts, scores, labels)


def prefix_lanes(values):
    lane = lax.broadcasted_iota(jnp.int32, values.shape, 1)
    step = 1
    while step < values.shape[1]:
        values = values + jnp.where(lane >= step, pltpu.roll(values, step, 1), 0.0)
        step *= 2
    return values


def compact(smaller_ref, counts_ref, lam_ref, child_ref, codes_ref, high_ref, low_ref, weight_ref, chunks_ref):
    query_dev, feats, slots = codes_ref.shape
    parents = smaller_ref.shape[0]
    lane = lax.broadcasted_iota(jnp.int32, (1, slots), 1)
    lam = jnp.concatenate([lam_ref[k].astype(jnp.float32) for k in range(lam_ref.shape[0])], axis=1)
    child = child_ref[...]
    parent = child >> 1
    wanted = jnp.zeros_like(child)
    for p in range(parents):
        wanted = jnp.where(parent == p, smaller_ref[p], wanted)
    usable = jnp.concatenate([(lane < counts_ref[q]).astype(jnp.int32) for q in range(query_dev)], axis=0) > 0
    live = ((child & 1) == wanted) & usable
    mine = live.astype(jnp.float32)
    rank = prefix_lanes(mine) - mine
    starts = []
    first = jnp.int32(0)
    for q in range(query_dev):
        starts.append([])
        for at in range(0, slots, BLOCK):
            starts[q].append(first)
            first = first + jnp.sum(mine[q : q + 1, at : at + BLOCK]).astype(jnp.int32)
    chunks = (first + CHUNK - 1) // CHUNK
    chunks_ref[0] = chunks

    def clear(t, carry):
        at = pl.ds(pl.multiple_of(t * CHUNK, CHUNK), CHUNK)
        low_ref[:, at] = jnp.zeros((feats, CHUNK), jnp.float32)
        weight_ref[:, at] = jnp.zeros((16, CHUNK), jnp.float32)
        return carry

    lax.fori_loop(0, chunks + 1, clear, 0)
    window = BLOCK + 128
    mark = lax.broadcasted_iota(jnp.int32, (window, 1), 0).astype(jnp.float32)
    one = jnp.ones((), jnp.bfloat16)
    zero = jnp.zeros((), jnp.bfloat16)
    local = lax.broadcasted_iota(jnp.int32, (parents, 1), 0)
    for q in range(query_dev):
        member = (parent[q : q + 1] == local) & live[q : q + 1]
        grad = jnp.where(member, lam[q : q + 1], 0.0)
        hess = jnp.where(member, lam[8 + q : 9 + q], 0.0)
        rows = jnp.concatenate((grad, hess), axis=0)
        moved = jnp.concatenate((codes_ref[q].astype(jnp.float32).astype(jnp.bfloat16), rows.astype(jnp.bfloat16)), axis=0)
        spot = jnp.where(live[q : q + 1], rank[q : q + 1] + starts[q][0].astype(jnp.float32), -1.0)
        for k, begin in enumerate(starts[q]):
            to = pl.multiple_of((begin // 128) * 128, 128)
            block = slice(k * BLOCK, (k + 1) * BLOCK)
            hot = jnp.where(spot[:, block] - to.astype(jnp.float32) == mark, one, zero)
            here = lax.dot_general(
                moved[:, block], hot, (((1,), (1,)), ((), ())), preferred_element_type=jnp.float32
            )
            low_ref[:, pl.ds(to, window)] += here[:feats]
            weight_ref[:, pl.ds(to, window)] += here[feats:]

    def split(t, carry):
        at = pl.ds(pl.multiple_of(t * CHUNK, CHUNK), CHUNK)
        code = low_ref[:, at]
        high = jnp.floor(code * (1.0 / LOWS))
        high_ref[:, at] = high
        low_ref[:, at] = code - high * LOWS
        return carry

    lax.fori_loop(0, chunks, split, 0)


def histogram_kernel(
    smaller_ref, counts_ref, lam_ref, child_ref, codes_ref, hist_ref,
    high_ref, low_ref, weight_ref, acc_ref, chunks_ref,
):
    feats = hist_ref.shape[0]

    @pl.when(pl.program_id(0) == 0)
    def _():
        compact(
            smaller_ref, counts_ref, lam_ref, child_ref, codes_ref,
            high_ref, low_ref, weight_ref, chunks_ref,
        )

    one = jnp.ones((), jnp.bfloat16)
    zero = jnp.zeros((), jnp.bfloat16)
    low_mark = lax.broadcasted_iota(jnp.int32, (LOWS, 1), 0).astype(jnp.float32).astype(jnp.bfloat16)
    base = pl.multiple_of(pl.program_id(0) * feats, 8)
    acc_ref[...] = jnp.zeros_like(acc_ref)

    def chunk(t, carry):
        at = pl.ds(pl.multiple_of(t * CHUNK, CHUNK), CHUNK)
        weight = weight_ref[:, at].astype(jnp.bfloat16)
        high_rows = high_ref[pl.ds(base, feats), at]
        low_rows = low_ref[pl.ds(base, feats), at]
        for part in range(feats // HIGHS):
            lhs = []
            rhs = []
            for f in range(part * HIGHS, part * HIGHS + HIGHS):
                high = jnp.broadcast_to(high_rows[f : f + 1], (16, CHUNK)).astype(jnp.bfloat16)
                low = jnp.broadcast_to(low_rows[f : f + 1], (LOWS, CHUNK)).astype(jnp.bfloat16)
                for h in range(HIGHS):
                    lhs.append(jnp.where(high == jnp.asarray(h, jnp.bfloat16), weight, zero))
                rhs.append(jnp.where(low == low_mark, one, zero))
            acc_ref[part] += lax.dot_general(
                jnp.concatenate(lhs, axis=0), jnp.concatenate(rhs, axis=0),
                (((1,), (1,)), ((), ())), preferred_element_type=jnp.float32,
            )
        return carry

    lax.fori_loop(0, chunks_ref[0], chunk, 0)
    wide = HIGHS * 16
    for f in range(feats):
        part, k = f // HIGHS, f % HIGHS
        pieces = [
            acc_ref[part, k * wide + h * 16 : k * wide + (h + 1) * 16, k * LOWS : (k + 1) * LOWS]
            for h in range(HIGHS)
        ]
        hist_ref[f] = jnp.concatenate(pieces, axis=1).astype(jnp.bfloat16)


def histograms(smaller, counts, lam, row_child, bin_codes):
    query_dev, feat_dev, slots = bin_codes.shape
    room = query_dev * slots + CHUNK
    smem = pl.BlockSpec(memory_space=pltpu.SMEM)

    def whole(array):
        return pl.BlockSpec(array.shape, lambda i: (0,) * array.ndim, pipeline_mode=pl.Buffered(1))

    return pl.pallas_call(
        histogram_kernel,
        grid=(feat_dev // FEATS,),
        out_shape=jax.ShapeDtypeStruct((feat_dev, 16, 256), jnp.bfloat16),
        in_specs=[smem, smem, whole(lam), whole(row_child), whole(bin_codes)],
        out_specs=pl.BlockSpec((FEATS, 16, 256), lambda i: (i, 0, 0)),
        scratch_shapes=[
            pltpu.VMEM((feat_dev, room), jnp.float32),
            pltpu.VMEM((feat_dev, room), jnp.float32),
            pltpu.VMEM((16, room), jnp.float32),
            pltpu.VMEM((FEATS // HIGHS, HIGHS * HIGHS * 16, 256), jnp.float32),
            pltpu.SMEM((1,), jnp.int32),
        ],
        name="histograms",
    )(smaller, counts, lam, row_child, bin_codes)


def gain_kernel(parts_ref, send_ref):
    rows, bins = parts_ref.shape[1:]
    built = jnp.sum(parts_ref[...].astype(jnp.float32), axis=0)
    below = lax.broadcasted_iota(jnp.int32, (bins, bins), 0)
    upto = lax.broadcasted_iota(jnp.int32, (bins, bins), 1)
    left = jnp.dot(
        built, (below <= upto).astype(jnp.float32),
        precision=lax.Precision.HIGHEST, preferred_element_type=jnp.float32,
    )
    threshold = lax.broadcasted_iota(jnp.int32, (8, bins), 1)
    best = jnp.full((8, 1), -jnp.inf, jnp.float32)
    for f in range(rows // 16):
        grad_left = left[f * 16 : f * 16 + 8]
        hess_left = left[f * 16 + 8 : f * 16 + 16]
        grad_total = grad_left[:, bins - 1 : bins]
        hess_total = hess_left[:, bins - 1 : bins]
        grad_right = grad_total - grad_left
        gain = (
            grad_left * grad_left / (hess_left + reg_lambda)
            + grad_right * grad_right / (hess_total - hess_left + reg_lambda)
            - grad_total * grad_total / (hess_total + reg_lambda)
        )
        gain = jnp.where(threshold < bins - 1, gain, -jnp.inf)
        best = jnp.maximum(best, jnp.max(gain, axis=1, keepdims=True))
    stacked = jnp.concatenate(
        (built, jnp.broadcast_to(best, (8, bins)), jnp.zeros((128 - rows - 8, bins), jnp.float32)), axis=0
    )
    send_ref[...] = stacked.T.reshape(send_ref.shape)


def children_kernel(smaller_ref, parts_ref, parent_ref, children_ref):
    sources, bin_span, lanes = parts_ref.shape
    parents, width = children_ref.shape[1:]
    group = width // sources
    column = lax.broadcasted_iota(jnp.int32, (sources, width), 1)
    source = lax.broadcasted_iota(jnp.int32, (sources, width), 0)
    spread = (column // group == source).astype(jnp.float32)
    rows = group * parents // 2
    row = lax.broadcasted_iota(jnp.int32, (rows, width), 0)
    col = lax.broadcasted_iota(jnp.int32, (rows, width), 1)
    match = (row // (2 * parents) == (col % group) // 4) & ((row // parents) % 2 == col % 2)
    pick_row = lax.broadcasted_iota(jnp.int32, (width // 2, width), 0)
    pick_col = lax.broadcasted_iota(jnp.int32, (width // 2, width), 1)
    pick = (pick_row == (pick_col // 4) * 2 + pick_col % 2).astype(jnp.float32)
    side = (lax.broadcasted_iota(jnp.int32, (parents, width), 1) // 2) % 2
    chosen = side == node_column(smaller_ref, parents)
    parent = jnp.dot(
        parent_ref[...].reshape(bin_span * parents, width // 2), pick,
        precision=lax.Precision.HIGHEST, preferred_element_type=jnp.float32,
    )
    for b in range(bin_span):
        wide = lax.dot_general(
            parts_ref[:, b, :], spread, (((0,), (0,)), ((), ())),
            precision=lax.Precision.HIGHEST, preferred_element_type=jnp.float32,
        )
        kept = jnp.where(match, wide[:rows], 0.0)
        built = jnp.sum(kept.reshape(rows // parents, parents, width), axis=0)
        children_ref[b] = jnp.where(chosen, built, parent[b * parents : (b + 1) * parents] - built)


def shards(scores, labels, counts, bin_codes, row_child, smaller, parent_hist):
    feat_dev = bin_codes.shape[1]
    bin_span, parents, _ = parent_hist.shape
    row_count = lax.axis_size("row")
    feat_count = lax.axis_size("feat")
    rows = feat_dev // row_count * 2 * parents
    bins = bin_span * row_count
    vmem = pl.BlockSpec(memory_space=pltpu.VMEM)
    smem = pl.BlockSpec(memory_space=pltpu.SMEM)
    lam = lax.all_to_all(lambdas(scores, labels, counts), "feat", 0, 0, tiled=True)
    hist = histograms(smaller, counts, lam, row_child, bin_codes)
    parts = lax.all_to_all(hist.reshape(row_count, rows, bins), "row", 0, 0, tiled=True)
    send = pl.pallas_call(
        gain_kernel,
        out_shape=jax.ShapeDtypeStruct((row_count, bin_span, 128), jnp.float32),
        in_specs=[vmem], out_specs=vmem, name="gains",
    )(parts)
    own = lax.all_to_all(send, "row", 0, 0, tiled=True)
    best = jnp.broadcast_to(jnp.max(own, axis=0)[None], (feat_count, bin_span, 128))
    best = jnp.max(lax.all_to_all(best, "feat", 0, 0, tiled=True), axis=0)
    children = pl.pallas_call(
        children_kernel,
        out_shape=jax.ShapeDtypeStruct((bin_span, parents, feat_dev * 4), jnp.float32),
        in_specs=[smem, vmem, vmem], out_specs=vmem, name="children",
    )(smaller, own, parent_hist)
    return children, best[0, rows : rows + parents]


def solution(mesh):
    placed = (
        P("row", None), P("row", None), P("row"), P("row", "feat", None),
        P("row", None), P(), P("row", None, "feat"),
    )
    return jax.shard_map(
        shards, mesh=mesh, in_specs=placed, out_specs=(P("row", None, "feat"), P()), check_vma=False
    )
```

```python
import jax
import jax.numpy as jnp
from jax import lax
from jax.experimental import pallas as pl
from jax.experimental.pallas import tpu as pltpu
from jax.sharding import PartitionSpec as P

levels = 5
reg_lambda = 1.0
SHARE = 128
STRETCH = 1024
HIGHS = 4
LOWS = 256 // HIGHS
CHUNK = 512
BLOCK = 256
FEATS = 96


def node_column(smaller_ref, parents):
    which = lax.broadcasted_iota(jnp.int32, (parents, 1), 0)
    column = jnp.zeros((parents, 1), jnp.int32)
    for p in range(parents):
        column = jnp.where(which == p, smaller_ref[p], column)
    return column


def count_column(counts_ref):
    which = lax.broadcasted_iota(jnp.int32, (8, 1), 0)
    column = jnp.zeros((8, 1), jnp.int32)
    for q in range(counts_ref.shape[0]):
        column = jnp.where(which == q, counts_ref[q], column)
    return column


def lambda_kernel(counts_ref, scores_ref, labels_ref, lam_ref, rows_ref, cols_ref, sums_ref):
    query_dev, slots = scores_ref.shape
    own = pl.multiple_of(lax.axis_index("feat") * SHARE, SHARE)
    position = lax.broadcasted_iota(jnp.int32, (8, slots), 1)
    discount = 1.0 / jnp.log2(position.astype(jnp.float32) + 2.0)
    counts = count_column(counts_ref)
    grade = labels_ref[...]
    usable = position[:query_dev] < counts[:query_dev]
    rows_ref[0:16, :] = jnp.zeros((16, slots), jnp.float32)
    rows_ref[0:query_dev, :] = jnp.where(usable, jnp.exp(scores_ref[...]), 0.0)
    rows_ref[8 : 8 + query_dev, :] = jnp.where(usable, jnp.exp2(grade.astype(jnp.float32)) - 1.0, -1.0)
    rows_ref[16:24, :] = discount
    cols_ref[...] = rows_ref[...].T
    sums_ref[...] = jnp.zeros_like(sums_ref)

    ideal = jnp.zeros((query_dev, slots), jnp.float32)
    ahead = jnp.zeros((query_dev, 1), jnp.int32)
    for c in range(levels - 1, 0, -1):
        here = jnp.sum(((grade == c) & usable).astype(jnp.float32), axis=1, keepdims=True).astype(jnp.int32)
        span = (position[:query_dev] >= ahead) & (position[:query_dev] < ahead + here)
        ideal = ideal + jnp.where(span, float(2**c - 1), 0.0)
        ahead = ahead + here
    ideal = jnp.sum(ideal * discount[:query_dev], axis=1, keepdims=True)
    inv_ideal = 1.0 / jnp.maximum(ideal, 1.0)

    for q in range(query_dev):
        count = counts_ref[q]
        e_i = rows_ref[q : q + 1, pl.ds(own, SHARE)]
        g_i = rows_ref[8 + q : 9 + q, pl.ds(own, SHARE)]
        d_i = rows_ref[16:17, pl.ds(own, SHARE)]

        def partners(jb, sums, q=q, e_i=e_i, g_i=g_i, d_i=d_i):
            grad_sum, hess_sum = sums
            at = pl.ds(pl.multiple_of(jb * STRETCH, STRETCH), STRETCH)
            e_j = cols_ref[at, q : q + 1]
            g_j = cols_ref[at, 8 + q : 9 + q]
            d_j = cols_ref[at, 16:17]
            inverse = 1.0 / (e_i + e_j)
            gain_gap = g_i - g_j
            higher = gain_gap > 0.0
            part = gain_gap * (jnp.abs(d_i - d_j) * inverse)
            grad = part * jnp.where(higher, e_j, e_i)
            hess = jnp.abs(grad) * (inverse * jnp.where(higher, e_i, e_j))
            grad_sum = grad_sum + jnp.sum(grad.reshape(STRETCH // 32, 32, SHARE), axis=0)
            hess_sum = hess_sum + jnp.sum(hess.reshape(STRETCH // 32, 32, SHARE), axis=0)
            return grad_sum, hess_sum

        zero = jnp.zeros((32, SHARE), jnp.float32)
        last = jnp.where(own < count, (count + STRETCH - 1) // STRETCH, 0)
        grad_sum, hess_sum = lax.fori_loop(0, last, partners, (zero, zero))
        sums_ref[q : q + 1, :] = -jnp.sum(grad_sum, axis=0, keepdims=True)
        sums_ref[8 + q : 9 + q, :] = jnp.sum(hess_sum, axis=0, keepdims=True)

    mine = own + lax.broadcasted_iota(jnp.int32, (query_dev, SHARE), 1) < counts[:query_dev]
    sums_ref[0:query_dev, :] = jnp.where(mine, sums_ref[0:query_dev, :] * inv_ideal, 0.0)
    sums_ref[8 : 8 + query_dev, :] = jnp.where(mine, sums_ref[8 : 8 + query_dev, :] * inv_ideal, 0.0)
    lam_ref[...] = jnp.broadcast_to(sums_ref[...].astype(jnp.bfloat16)[None], lam_ref.shape)


def lambdas(scores, labels, counts):
    query_dev, slots = scores.shape
    vmem = pl.BlockSpec(memory_space=pltpu.VMEM)
    smem = pl.BlockSpec(memory_space=pltpu.SMEM)
    return pl.pallas_call(
        lambda_kernel,
        out_shape=jax.ShapeDtypeStruct((slots // SHARE, 16, SHARE), jnp.bfloat16),
        in_specs=[smem, vmem, vmem],
        out_specs=vmem,
        scratch_shapes=[
            pltpu.VMEM((24, slots), jnp.float32),
            pltpu.VMEM((slots, 24), jnp.float32),
            pltpu.VMEM((16, SHARE), jnp.float32),
        ],
        name="lambdas",
    )(counts, scores, labels)


def prefix_lanes(values):
    lane = lax.broadcasted_iota(jnp.int32, values.shape, 1)
    step = 1
    while step < values.shape[1]:
        values = values + jnp.where(lane >= step, pltpu.roll(values, step, 1), 0.0)
        step *= 2
    return values


def compact(smaller_ref, counts_ref, lam_ref, child_ref, codes_ref, high_ref, low_ref, weight_ref, chunks_ref):
    query_dev, feats, slots = codes_ref.shape
    parents = smaller_ref.shape[0]
    lane = lax.broadcasted_iota(jnp.int32, (1, slots), 1)
    lam = jnp.concatenate([lam_ref[k].astype(jnp.float32) for k in range(lam_ref.shape[0])], axis=1)
    child = child_ref[...]
    parent = child >> 1
    wanted = jnp.zeros_like(child)
    for p in range(parents):
        wanted = jnp.where(parent == p, smaller_ref[p], wanted)
    usable = jnp.concatenate([(lane < counts_ref[q]).astype(jnp.int32) for q in range(query_dev)], axis=0) > 0
    live = ((child & 1) == wanted) & usable
    mine = live.astype(jnp.float32)
    rank = prefix_lanes(mine) - mine
    starts = []
    first = jnp.int32(0)
    for q in range(query_dev):
        starts.append([])
        for at in range(0, slots, BLOCK):
            starts[q].append(first)
            first = first + jnp.sum(mine[q : q + 1, at : at + BLOCK]).astype(jnp.int32)
    chunks = (first + CHUNK - 1) // CHUNK
    chunks_ref[0] = chunks

    def clear(t, carry):
        at = pl.ds(pl.multiple_of(t * CHUNK, CHUNK), CHUNK)
        low_ref[:, at] = jnp.zeros((feats, CHUNK), jnp.float32)
        weight_ref[:, at] = jnp.zeros((16, CHUNK), jnp.float32)
        return carry

    lax.fori_loop(0, chunks + 1, clear, 0)
    window = BLOCK + 128
    mark = lax.broadcasted_iota(jnp.int32, (window, 1), 0).astype(jnp.float32)
    one = jnp.ones((), jnp.bfloat16)
    zero = jnp.zeros((), jnp.bfloat16)
    local = lax.broadcasted_iota(jnp.int32, (parents, 1), 0)
    for q in range(query_dev):
        member = (parent[q : q + 1] == local) & live[q : q + 1]
        grad = jnp.where(member, lam[q : q + 1], 0.0)
        hess = jnp.where(member, lam[8 + q : 9 + q], 0.0)
        rows = jnp.concatenate((grad, hess), axis=0)
        moved = jnp.concatenate((codes_ref[q].astype(jnp.float32).astype(jnp.bfloat16), rows.astype(jnp.bfloat16)), axis=0)
        spot = jnp.where(live[q : q + 1], rank[q : q + 1] + starts[q][0].astype(jnp.float32), -1.0)
        for k, begin in enumerate(starts[q]):
            to = pl.multiple_of((begin // 128) * 128, 128)
            block = slice(k * BLOCK, (k + 1) * BLOCK)
            hot = jnp.where(spot[:, block] - to.astype(jnp.float32) == mark, one, zero)
            here = lax.dot_general(
                moved[:, block], hot, (((1,), (1,)), ((), ())), preferred_element_type=jnp.float32
            )
            low_ref[:, pl.ds(to, window)] += here[:feats]
            weight_ref[:, pl.ds(to, window)] += here[feats:]

    def split(t, carry):
        at = pl.ds(pl.multiple_of(t * CHUNK, CHUNK), CHUNK)
        code = low_ref[:, at]
        high = jnp.floor(code * (1.0 / LOWS))
        high_ref[:, at] = high
        low_ref[:, at] = code - high * LOWS
        return carry

    lax.fori_loop(0, chunks, split, 0)


def histogram_kernel(
    smaller_ref, counts_ref, lam_ref, child_ref, codes_ref, hist_ref,
    high_ref, low_ref, weight_ref, acc_ref, chunks_ref,
):
    feats = hist_ref.shape[0]

    @pl.when(pl.program_id(0) == 0)
    def _():
        compact(
            smaller_ref, counts_ref, lam_ref, child_ref, codes_ref,
            high_ref, low_ref, weight_ref, chunks_ref,
        )

    one = jnp.ones((), jnp.bfloat16)
    zero = jnp.zeros((), jnp.bfloat16)
    low_mark = lax.broadcasted_iota(jnp.int32, (LOWS, 1), 0).astype(jnp.float32).astype(jnp.bfloat16)
    base = pl.multiple_of(pl.program_id(0) * feats, 8)
    acc_ref[...] = jnp.zeros_like(acc_ref)

    def chunk(t, carry):
        at = pl.ds(pl.multiple_of(t * CHUNK, CHUNK), CHUNK)
        weight = weight_ref[:, at].astype(jnp.bfloat16)
        high_rows = high_ref[pl.ds(base, feats), at]
        low_rows = low_ref[pl.ds(base, feats), at]
        for part in range(feats // HIGHS):
            lhs = []
            rhs = []
            for f in range(part * HIGHS, part * HIGHS + HIGHS):
                high = jnp.broadcast_to(high_rows[f : f + 1], (16, CHUNK)).astype(jnp.bfloat16)
                low = jnp.broadcast_to(low_rows[f : f + 1], (LOWS, CHUNK)).astype(jnp.bfloat16)
                for h in range(HIGHS):
                    lhs.append(jnp.where(high == jnp.asarray(h, jnp.bfloat16), weight, zero))
                rhs.append(jnp.where(low == low_mark, one, zero))
            acc_ref[part] += lax.dot_general(
                jnp.concatenate(lhs, axis=0), jnp.concatenate(rhs, axis=0),
                (((1,), (1,)), ((), ())), preferred_element_type=jnp.float32,
            )
        return carry

    lax.fori_loop(0, chunks_ref[0], chunk, 0)
    wide = HIGHS * 16
    for f in range(feats):
        part, k = f // HIGHS, f % HIGHS
        pieces = [
            acc_ref[part, k * wide + h * 16 : k * wide + (h + 1) * 16, k * LOWS : (k + 1) * LOWS]
            for h in range(HIGHS)
        ]
        hist_ref[f] = jnp.concatenate(pieces, axis=1).astype(jnp.bfloat16)


def histograms(smaller, counts, lam, row_child, bin_codes):
    query_dev, feat_dev, slots = bin_codes.shape
    room = query_dev * slots + CHUNK
    smem = pl.BlockSpec(memory_space=pltpu.SMEM)

    def whole(array):
        return pl.BlockSpec(array.shape, lambda i: (0,) * array.ndim, pipeline_mode=pl.Buffered(1))

    return pl.pallas_call(
        histogram_kernel,
        grid=(feat_dev // FEATS,),
        out_shape=jax.ShapeDtypeStruct((feat_dev, 16, 256), jnp.bfloat16),
        in_specs=[smem, smem, whole(lam), whole(row_child), whole(bin_codes)],
        out_specs=pl.BlockSpec((FEATS, 16, 256), lambda i: (i, 0, 0)),
        scratch_shapes=[
            pltpu.VMEM((feat_dev, room), jnp.float32),
            pltpu.VMEM((feat_dev, room), jnp.float32),
            pltpu.VMEM((16, room), jnp.float32),
            pltpu.VMEM((FEATS // HIGHS, HIGHS * HIGHS * 16, 256), jnp.float32),
            pltpu.SMEM((1,), jnp.int32),
        ],
        name="histograms",
    )(smaller, counts, lam, row_child, bin_codes)


def gain_kernel(parts_ref, send_ref):
    rows, bins = parts_ref.shape[1:]
    built = jnp.sum(parts_ref[...].astype(jnp.float32), axis=0)
    below = lax.broadcasted_iota(jnp.int32, (bins, bins), 0)
    upto = lax.broadcasted_iota(jnp.int32, (bins, bins), 1)
    left = jnp.dot(
        built, (below <= upto).astype(jnp.float32),
        precision=lax.Precision.HIGHEST, preferred_element_type=jnp.float32,
    )
    threshold = lax.broadcasted_iota(jnp.int32, (8, bins), 1)
    best = jnp.full((8, 1), -jnp.inf, jnp.float32)
    for f in range(rows // 16):
        grad_left = left[f * 16 : f * 16 + 8]
        hess_left = left[f * 16 + 8 : f * 16 + 16]
        grad_total = grad_left[:, bins - 1 : bins]
        hess_total = hess_left[:, bins - 1 : bins]
        grad_right = grad_total - grad_left
        gain = (
            grad_left * grad_left / (hess_left + reg_lambda)
            + grad_right * grad_right / (hess_total - hess_left + reg_lambda)
            - grad_total * grad_total / (hess_total + reg_lambda)
        )
        gain = jnp.where(threshold < bins - 1, gain, -jnp.inf)
        best = jnp.maximum(best, jnp.max(gain, axis=1, keepdims=True))
    stacked = jnp.concatenate(
        (built, jnp.broadcast_to(best, (8, bins)), jnp.zeros((128 - rows - 8, bins), jnp.float32)), axis=0
    )
    send_ref[...] = stacked.T.reshape(send_ref.shape)


def children_kernel(smaller_ref, parts_ref, parent_ref, children_ref):
    sources, bin_span, lanes = parts_ref.shape
    parents, width = children_ref.shape[1:]
    group = width // sources
    column = lax.broadcasted_iota(jnp.int32, (sources, width), 1)
    source = lax.broadcasted_iota(jnp.int32, (sources, width), 0)
    spread = (column // group == source).astype(jnp.float32)
    rows = group * parents // 2
    row = lax.broadcasted_iota(jnp.int32, (rows, width), 0)
    col = lax.broadcasted_iota(jnp.int32, (rows, width), 1)
    match = (row // (2 * parents) == (col % group) // 4) & ((row // parents) % 2 == col % 2)
    pick_row = lax.broadcasted_iota(jnp.int32, (width // 2, width), 0)
    pick_col = lax.broadcasted_iota(jnp.int32, (width // 2, width), 1)
    pick = (pick_row == (pick_col // 4) * 2 + pick_col % 2).astype(jnp.float32)
    side = (lax.broadcasted_iota(jnp.int32, (parents, width), 1) // 2) % 2
    chosen = side == node_column(smaller_ref, parents)
    parent = jnp.dot(
        parent_ref[...].reshape(bin_span * parents, width // 2), pick,
        precision=lax.Precision.HIGHEST, preferred_element_type=jnp.float32,
    )
    for b in range(bin_span):
        wide = lax.dot_general(
            parts_ref[:, b, :], spread, (((0,), (0,)), ((), ())),
            precision=lax.Precision.HIGHEST, preferred_element_type=jnp.float32,
        )
        kept = jnp.where(match, wide[:rows], 0.0)
        built = jnp.sum(kept.reshape(rows // parents, parents, width), axis=0)
        children_ref[b] = jnp.where(chosen, built, parent[b * parents : (b + 1) * parents] - built)


def shards(scores, labels, counts, bin_codes, row_child, smaller, parent_hist):
    feat_dev = bin_codes.shape[1]
    bin_span, parents, _ = parent_hist.shape
    row_count = lax.axis_size("row")
    feat_count = lax.axis_size("feat")
    rows = feat_dev // row_count * 2 * parents
    bins = bin_span * row_count
    vmem = pl.BlockSpec(memory_space=pltpu.VMEM)
    smem = pl.BlockSpec(memory_space=pltpu.SMEM)
    lam = lax.all_to_all(lambdas(scores, labels, counts), "feat", 0, 0, tiled=True)
    hist = histograms(smaller, counts, lam, row_child, bin_codes)
    parts = lax.all_to_all(hist.reshape(row_count, rows, bins), "row", 0, 0, tiled=True)
    send = pl.pallas_call(
        gain_kernel,
        out_shape=jax.ShapeDtypeStruct((row_count, bin_span, 128), jnp.float32),
        in_specs=[vmem], out_specs=vmem, name="gains",
    )(parts)
    own = lax.all_to_all(send, "row", 0, 0, tiled=True)
    best = jnp.broadcast_to(jnp.max(own, axis=0)[None], (feat_count, bin_span, 128))
    best = jnp.max(lax.all_to_all(best, "feat", 0, 0, tiled=True), axis=0)
    children = pl.pallas_call(
        children_kernel,
        out_shape=jax.ShapeDtypeStruct((bin_span, parents, feat_dev * 4), jnp.float32),
        in_specs=[smem, vmem, vmem], out_specs=vmem, name="children",
    )(smaller, own, parent_hist)
    return children, best[0, rows : rows + parents]


def solution(mesh):
    placed = (
        P("row", None), P("row", None), P("row"), P("row", "feat", None),
        P("row", None), P(), P("row", None, "feat"),
    )
    return jax.shard_map(
        shards, mesh=mesh, in_specs=placed, out_specs=(P("row", None, "feat"), P()), check_vma=False
    )
```

```python
import jax
import jax.numpy as jnp
from jax import lax
from jax.experimental import pallas as pl
from jax.experimental.pallas import tpu as pltpu
from jax.sharding import PartitionSpec as P

levels = 5
reg_lambda = 1.0
SHARE = 128
STRETCH = 1024
GROUPS = 4
HIGHS = 8
LOWS = 256 // HIGHS
CHUNK = 256
BLOCK = 512


def node_column(smaller_ref, parents):
    which = lax.broadcasted_iota(jnp.int32, (parents, 1), 0)
    column = jnp.zeros((parents, 1), jnp.int32)
    for p in range(parents):
        column = jnp.where(which == p, smaller_ref[p], column)
    return column


def count_column(counts_ref):
    which = lax.broadcasted_iota(jnp.int32, (8, 1), 0)
    column = jnp.zeros((8, 1), jnp.int32)
    for q in range(counts_ref.shape[0]):
        column = jnp.where(which == q, counts_ref[q], column)
    return column


def lambda_kernel(counts_ref, scores_ref, labels_ref, lam_ref, rows_ref, cols_ref, sums_ref):
    query_dev, slots = scores_ref.shape
    own = pl.multiple_of(lax.axis_index("feat") * SHARE, SHARE)
    position = lax.broadcasted_iota(jnp.int32, (8, slots), 1)
    discount = 1.0 / jnp.log2(position.astype(jnp.float32) + 2.0)
    counts = count_column(counts_ref)
    grade = labels_ref[...]
    usable = position[:query_dev] < counts[:query_dev]
    rows_ref[0:16, :] = jnp.zeros((16, slots), jnp.float32)
    rows_ref[0:query_dev, :] = jnp.where(usable, jnp.exp(scores_ref[...]), 0.0)
    rows_ref[8 : 8 + query_dev, :] = jnp.where(usable, jnp.exp2(grade.astype(jnp.float32)) - 1.0, -1.0)
    rows_ref[16:24, :] = discount
    cols_ref[...] = rows_ref[...].T
    sums_ref[...] = jnp.zeros_like(sums_ref)

    ideal = jnp.zeros((query_dev, slots), jnp.float32)
    ahead = jnp.zeros((query_dev, 1), jnp.int32)
    for c in range(levels - 1, 0, -1):
        here = jnp.sum(((grade == c) & usable).astype(jnp.float32), axis=1, keepdims=True).astype(jnp.int32)
        span = (position[:query_dev] >= ahead) & (position[:query_dev] < ahead + here)
        ideal = ideal + jnp.where(span, float(2**c - 1), 0.0)
        ahead = ahead + here
    ideal = jnp.sum(ideal * discount[:query_dev], axis=1, keepdims=True)
    inv_ideal = 1.0 / jnp.maximum(ideal, 1.0)

    for q in range(query_dev):
        count = counts_ref[q]
        e_i = rows_ref[q : q + 1, pl.ds(own, SHARE)]
        g_i = rows_ref[8 + q : 9 + q, pl.ds(own, SHARE)]
        d_i = rows_ref[16:17, pl.ds(own, SHARE)]

        def partners(jb, sums, q=q, e_i=e_i, g_i=g_i, d_i=d_i):
            grad_sum, hess_sum = sums
            at = pl.ds(pl.multiple_of(jb * STRETCH, STRETCH), STRETCH)
            e_j = cols_ref[at, q : q + 1]
            g_j = cols_ref[at, 8 + q : 9 + q]
            d_j = cols_ref[at, 16:17]
            inverse = 1.0 / (e_i + e_j)
            gain_gap = g_i - g_j
            higher = gain_gap > 0.0
            part = gain_gap * (jnp.abs(d_i - d_j) * inverse)
            grad = part * jnp.where(higher, e_j, e_i)
            hess = jnp.abs(grad) * (inverse * jnp.where(higher, e_i, e_j))
            grad_sum = grad_sum + jnp.sum(grad.reshape(STRETCH // 32, 32, SHARE), axis=0)
            hess_sum = hess_sum + jnp.sum(hess.reshape(STRETCH // 32, 32, SHARE), axis=0)
            return grad_sum, hess_sum

        zero = jnp.zeros((32, SHARE), jnp.float32)
        last = jnp.where(own < count, (count + STRETCH - 1) // STRETCH, 0)
        grad_sum, hess_sum = lax.fori_loop(0, last, partners, (zero, zero))
        sums_ref[q : q + 1, :] = -jnp.sum(grad_sum, axis=0, keepdims=True)
        sums_ref[8 + q : 9 + q, :] = jnp.sum(hess_sum, axis=0, keepdims=True)

    mine = own + lax.broadcasted_iota(jnp.int32, (query_dev, SHARE), 1) < counts[:query_dev]
    sums_ref[0:query_dev, :] = jnp.where(mine, sums_ref[0:query_dev, :] * inv_ideal, 0.0)
    sums_ref[8 : 8 + query_dev, :] = jnp.where(mine, sums_ref[8 : 8 + query_dev, :] * inv_ideal, 0.0)
    lam_ref[...] = jnp.broadcast_to(sums_ref[...].astype(jnp.bfloat16)[None], lam_ref.shape)


def lambdas(scores, labels, counts):
    query_dev, slots = scores.shape
    vmem = pl.BlockSpec(memory_space=pltpu.VMEM)
    smem = pl.BlockSpec(memory_space=pltpu.SMEM)
    return pl.pallas_call(
        lambda_kernel,
        out_shape=jax.ShapeDtypeStruct((slots // SHARE, 16, SHARE), jnp.bfloat16),
        in_specs=[smem, vmem, vmem],
        out_specs=vmem,
        scratch_shapes=[
            pltpu.VMEM((24, slots), jnp.float32),
            pltpu.VMEM((slots, 24), jnp.float32),
            pltpu.VMEM((16, SHARE), jnp.float32),
        ],
        name="lambdas",
    )(counts, scores, labels)


def prefix_lanes(values):
    lane = lax.broadcasted_iota(jnp.int32, values.shape, 1)
    step = 1
    while step < values.shape[1]:
        values = values + jnp.where(lane >= step, pltpu.roll(values, step, 1), 0.0)
        step *= 2
    return values


def compact(
    smaller_ref, counts_ref, lam_ref, child_ref, codes_ref,
    high_ref, low_ref, weight_ref, moved_ref, spot_ref, chunks_ref,
):
    query_dev, feats, slots = codes_ref.shape
    parents = smaller_ref.shape[0]
    per_group = parents // GROUPS
    blocks = slots // BLOCK
    lam = jnp.concatenate([lam_ref[k].astype(jnp.float32) for k in range(lam_ref.shape[0])], axis=1)
    child = child_ref[...]
    parent = child >> 1
    wanted = jnp.zeros_like(child)
    for p in range(parents):
        wanted = jnp.where(parent == p, smaller_ref[p], wanted)
    position = lax.broadcasted_iota(jnp.int32, child.shape, 1)
    usable = position < count_column(counts_ref)[:query_dev]
    live = ((child & 1) == wanted) & usable
    owner = jnp.where(live, parent // per_group, -1)
    numbers = {}
    ranks = []
    for g in range(0, GROUPS, 2):
        pair = jnp.where(owner == g, 1, jnp.where(owner == g + 1, 4096, 0)).astype(jnp.float32)
        for q in range(query_dev):
            for k in range(blocks):
                total = jnp.sum(pair[q : q + 1, k * BLOCK : (k + 1) * BLOCK]).astype(jnp.int32)
                numbers[g, q, k] = total & 4095
                numbers[g + 1, q, k] = total >> 12
        packed = (prefix_lanes(pair) - pair).astype(jnp.int32)
        ranks += [(packed & 4095).astype(jnp.float32), (packed >> 12).astype(jnp.float32)]
    starts = {}
    base = jnp.int32(0)
    crowded = jnp.int32(0)
    which = lax.broadcasted_iota(jnp.int32, (8, 1), 0)
    for g in range(GROUPS):
        first = base
        opening = jnp.zeros((8, 1), jnp.float32)
        for q in range(query_dev):
            opening = jnp.where(which == q, first.astype(jnp.float32), opening)
            for k in range(blocks):
                starts[g, q, k] = first
                first = first + numbers[g, q, k]
                crowded = jnp.maximum(crowded, numbers[g, q, k])
        spot_ref[g, 0:query_dev, :] = jnp.where(owner == g, ranks[g] + opening[:query_dev], -1.0)
        chunks = (first - base + CHUNK - 1) // CHUNK
        chunks_ref[g, 0] = base // CHUNK
        chunks_ref[g, 1] = chunks
        base = base + chunks * CHUNK

    def clear(t, carry):
        at = pl.ds(pl.multiple_of(t * CHUNK, CHUNK), CHUNK)
        low_ref[:, at] = jnp.zeros((feats, CHUNK), jnp.float32)
        weight_ref[:, at] = jnp.zeros((16, CHUNK), jnp.float32)
        return carry

    lax.fori_loop(0, base // CHUNK, clear, 0)
    local = lax.broadcasted_iota(jnp.int32, (per_group, 1), 0)
    for q in range(query_dev):
        member = ((parent[q : q + 1] % per_group) == local) & live[q : q + 1]
        grad = jnp.where(member, lam[q : q + 1], 0.0)
        hess = jnp.where(member, lam[8 + q : 9 + q], 0.0)
        rows = jnp.concatenate((grad, hess) * GROUPS, axis=0)
        moved_ref[q, 0:feats, :] = codes_ref[q].astype(jnp.float32).astype(jnp.bfloat16)
        moved_ref[q, feats : feats + 16, :] = rows.astype(jnp.bfloat16)
    mark = lax.broadcasted_iota(jnp.int32, (128, 1), 0).astype(jnp.float32)
    lane = lax.broadcasted_iota(jnp.int32, (1, 128), 1)
    one = jnp.ones((), jnp.bfloat16)
    zero = jnp.zeros((), jnp.bfloat16)

    def place(skip):
        for q in range(query_dev):
            for k in range(blocks):
                block = slice(k * BLOCK, (k + 1) * BLOCK)
                moved = moved_ref[q, :, block]
                for g in range(GROUPS):
                    begin = starts[g, q, k]
                    to = pl.multiple_of((begin // 128) * 128, 128)
                    offset = begin - to
                    ahead = spot_ref[g, q : q + 1, block] - (to + skip).astype(jnp.float32)
                    shift = offset.astype(jnp.float32)
                    here = jnp.where((ahead >= shift) & (ahead < shift + 128.0), ahead, -1.0)
                    here = jnp.where(here >= 128.0, here - 128.0, here)
                    hot = jnp.where(here == mark, one, zero)
                    out = lax.dot_general(
                        moved, hot, (((1,), (1,)), ((), ())), preferred_element_type=jnp.float32
                    )
                    now = jnp.where(lane >= offset, out, 0.0)
                    then = jnp.where(lane >= offset, 0.0, out)
                    for add, start in ((now, to + skip), (then, to + skip + 128)):
                        at = pl.ds(pl.multiple_of(start, 128), 128)
                        low_ref[:, at] += add[:feats]
                        weight_ref[:, at] += add[feats:]

    def turn(t, carry):
        place(t * 128)
        return carry

    lax.fori_loop(0, (crowded + 127) // 128, turn, 0)

    def split(t, carry):
        at = pl.ds(pl.multiple_of(t * CHUNK, CHUNK), CHUNK)
        code = low_ref[:, at]
        high = jnp.floor(code * (1.0 / LOWS))
        high_ref[:, at] = high
        low_ref[:, at] = code - high * LOWS
        return carry

    lax.fori_loop(0, base // CHUNK, split, 0)


def histogram_kernel(
    smaller_ref, counts_ref, lam_ref, child_ref, codes_ref, hist_ref,
    high_ref, low_ref, weight_ref, moved_ref, spot_ref, acc_ref, chunks_ref,
):
    feats = hist_ref.shape[0]
    compact(
        smaller_ref, counts_ref, lam_ref, child_ref, codes_ref,
        high_ref, low_ref, weight_ref, moved_ref, spot_ref, chunks_ref,
    )
    kinds = 16 // GROUPS
    wide = HIGHS * kinds
    one = jnp.ones((), jnp.bfloat16)
    zero = jnp.zeros((), jnp.bfloat16)
    low_mark = lax.broadcasted_iota(jnp.int32, (LOWS, 1), 0).astype(jnp.float32).astype(jnp.bfloat16)
    slot = lax.broadcasted_iota(jnp.int32, (16, 1), 0) // kinds
    lane = lax.broadcasted_iota(jnp.int32, (1, 128), 1)
    acc_ref[...] = jnp.zeros_like(acc_ref)
    for g in range(GROUPS):

        def chunk(t, carry, g=g):
            at = pl.ds(pl.multiple_of((chunks_ref[g, 0] + t) * CHUNK, CHUNK), CHUNK)
            weight = weight_ref[:, at].astype(jnp.bfloat16)
            for first in range(0, feats, HIGHS):
                lhs = []
                rhs = [None] * HIGHS
                for k in range(HIGHS):
                    f = first + k
                    high = jnp.broadcast_to(high_ref[f : f + 1, at], (16, CHUNK)).astype(jnp.bfloat16)
                    low = jnp.broadcast_to(low_ref[f : f + 1, at], (LOWS, CHUNK)).astype(jnp.bfloat16)
                    for j in range(wide // 16):
                        marks = (slot + j * GROUPS).astype(jnp.float32).astype(jnp.bfloat16)
                        lhs.append(jnp.where(high == marks, weight, zero))
                    rhs[k // GROUPS * GROUPS + (k + g) % GROUPS] = jnp.where(low == low_mark, one, zero)
                out = lax.dot_general(
                    jnp.concatenate(lhs, axis=0), jnp.concatenate(rhs, axis=0),
                    (((1,), (1,)), ((), ())), preferred_element_type=jnp.float32,
                )
                for k in range(HIGHS):
                    half = k // GROUPS * 128
                    mine = lane // LOWS == (k + g) % GROUPS
                    acc_ref[first + k] += jnp.where(
                        mine, out[k * wide : (k + 1) * wide, half : half + 128], 0.0
                    )
            return carry

        lax.fori_loop(0, chunks_ref[g, 1], chunk, 0)
    hist_ref[...] = acc_ref[...].astype(jnp.bfloat16)


def histograms(smaller, counts, lam, row_child, bin_codes):
    query_dev, feat_dev, slots = bin_codes.shape
    room = query_dev * slots + GROUPS * CHUNK + BLOCK + 256
    vmem = pl.BlockSpec(memory_space=pltpu.VMEM)
    smem = pl.BlockSpec(memory_space=pltpu.SMEM)
    wide = HIGHS * 16 // GROUPS
    return pl.pallas_call(
        histogram_kernel,
        out_shape=jax.ShapeDtypeStruct((feat_dev, wide, 128), jnp.bfloat16),
        in_specs=[smem, smem, vmem, vmem, vmem],
        out_specs=vmem,
        scratch_shapes=[
            pltpu.VMEM((feat_dev, room), jnp.float32),
            pltpu.VMEM((feat_dev, room), jnp.float32),
            pltpu.VMEM((16, room), jnp.float32),
            pltpu.VMEM((query_dev, feat_dev + 16, slots), jnp.bfloat16),
            pltpu.VMEM((GROUPS, 8, slots), jnp.float32),
            pltpu.VMEM((feat_dev, wide, 128), jnp.float32),
            pltpu.SMEM((GROUPS, 2), jnp.int32),
        ],
        name="histograms",
    )(smaller, counts, lam, row_child, bin_codes)


def gain_kernel(parts_ref, send_ref):
    wide = HIGHS * 16 // GROUPS
    feats = parts_ref.shape[1] // wide
    bins = HIGHS * LOWS
    kinds = 16 // GROUPS
    summed = jnp.sum(parts_ref[...].astype(jnp.float32), axis=0)
    built = []
    for f in range(feats):
        turn = (lax.axis_index("row") * feats + f) % GROUPS
        block = pltpu.roll(summed[f * wide : (f + 1) * wide], (GROUPS - turn) * LOWS % 128, 1)
        stats = ([], [])
        for g in range(GROUPS):
            pieces = [block[h * kinds : (h + 1) * kinds, g * LOWS : (g + 1) * LOWS] for h in range(HIGHS)]
            both = jnp.concatenate(pieces, axis=1)
            stats[0].append(both[: kinds // 2])
            stats[1].append(both[kinds // 2 :])
        built += stats[0] + stats[1]
    built = jnp.concatenate(built, axis=0)
    rows = built.shape[0]
    below = lax.broadcasted_iota(jnp.int32, (bins, bins), 0)
    upto = lax.broadcasted_iota(jnp.int32, (bins, bins), 1)
    left = jnp.dot(
        built, (below <= upto).astype(jnp.float32),
        precision=lax.Precision.HIGHEST, preferred_element_type=jnp.float32,
    )
    threshold = lax.broadcasted_iota(jnp.int32, (8, bins), 1)
    best = jnp.full((8, 1), -jnp.inf, jnp.float32)
    for f in range(feats):
        grad_left = left[f * 16 : f * 16 + 8]
        hess_left = left[f * 16 + 8 : f * 16 + 16]
        grad_total = grad_left[:, bins - 1 : bins]
        hess_total = hess_left[:, bins - 1 : bins]
        grad_right = grad_total - grad_left
        gain = (
            grad_left * grad_left / (hess_left + reg_lambda)
            + grad_right * grad_right / (hess_total - hess_left + reg_lambda)
            - grad_total * grad_total / (hess_total + reg_lambda)
        )
        gain = jnp.where(threshold < bins - 1, gain, -jnp.inf)
        best = jnp.maximum(best, jnp.max(gain, axis=1, keepdims=True))
    stacked = jnp.concatenate(
        (built, jnp.broadcast_to(best, (8, bins)), jnp.zeros((128 - rows - 8, bins), jnp.float32)), axis=0
    )
    send_ref[...] = stacked.T.reshape(send_ref.shape)


def children_kernel(smaller_ref, parts_ref, parent_ref, children_ref):
    sources, bin_span, lanes = parts_ref.shape
    parents, width = children_ref.shape[1:]
    group = width // sources
    column = lax.broadcasted_iota(jnp.int32, (sources, width), 1)
    source = lax.broadcasted_iota(jnp.int32, (sources, width), 0)
    spread = (column // group == source).astype(jnp.float32)
    rows = group * parents // 2
    row = lax.broadcasted_iota(jnp.int32, (rows, width), 0)
    col = lax.broadcasted_iota(jnp.int32, (rows, width), 1)
    match = (row // (2 * parents) == (col % group) // 4) & ((row // parents) % 2 == col % 2)
    pick_row = lax.broadcasted_iota(jnp.int32, (width // 2, width), 0)
    pick_col = lax.broadcasted_iota(jnp.int32, (width // 2, width), 1)
    pick = (pick_row == (pick_col // 4) * 2 + pick_col % 2).astype(jnp.float32)
    side = (lax.broadcasted_iota(jnp.int32, (parents, width), 1) // 2) % 2
    chosen = side == node_column(smaller_ref, parents)
    parent = jnp.dot(
        parent_ref[...].reshape(bin_span * parents, width // 2), pick,
        precision=lax.Precision.HIGHEST, preferred_element_type=jnp.float32,
    )
    for b in range(bin_span):
        wide = lax.dot_general(
            parts_ref[:, b, :], spread, (((0,), (0,)), ((), ())),
            precision=lax.Precision.HIGHEST, preferred_element_type=jnp.float32,
        )
        kept = jnp.where(match, wide[:rows], 0.0)
        built = jnp.sum(kept.reshape(rows // parents, parents, width), axis=0)
        children_ref[b] = jnp.where(chosen, built, parent[b * parents : (b + 1) * parents] - built)


def shards(scores, labels, counts, bin_codes, row_child, smaller, parent_hist):
    feat_dev = bin_codes.shape[1]
    bin_span, parents, _ = parent_hist.shape
    row_count = lax.axis_size("row")
    feat_count = lax.axis_size("feat")
    rows = feat_dev // row_count * 2 * parents
    bins = bin_span * row_count
    vmem = pl.BlockSpec(memory_space=pltpu.VMEM)
    smem = pl.BlockSpec(memory_space=pltpu.SMEM)
    lam = lax.all_to_all(lambdas(scores, labels, counts), "feat", 0, 0, tiled=True)
    hist = histograms(smaller, counts, lam, row_child, bin_codes)
    parts = lax.all_to_all(hist.reshape(row_count, -1, 128), "row", 0, 0, tiled=True)
    send = pl.pallas_call(
        gain_kernel,
        out_shape=jax.ShapeDtypeStruct((row_count, bin_span, 128), jnp.float32),
        in_specs=[vmem], out_specs=vmem, name="gains",
    )(parts)
    own = lax.all_to_all(send, "row", 0, 0, tiled=True)
    best = jnp.broadcast_to(jnp.max(own, axis=0)[None], (feat_count, bin_span, 128))
    best = jnp.max(lax.all_to_all(best, "feat", 0, 0, tiled=True), axis=0)
    children = pl.pallas_call(
        children_kernel,
        out_shape=jax.ShapeDtypeStruct((bin_span, parents, feat_dev * 4), jnp.float32),
        in_specs=[smem, vmem, vmem], out_specs=vmem, name="children",
    )(smaller, own, parent_hist)
    return children, best[0, rows : rows + parents]


def solution(mesh):
    placed = (
        P("row", None), P("row", None), P("row"), P("row", "feat", None),
        P("row", None), P(), P("row", None, "feat"),
    )
    return jax.shard_map(
        shards, mesh=mesh, in_specs=placed, out_specs=(P("row", None, "feat"), P()), check_vma=False
    )
```

```python
import jax
import jax.numpy as jnp
from jax import lax
from jax.experimental import pallas as pl
from jax.experimental.pallas import tpu as pltpu
from jax.sharding import PartitionSpec as P

levels = 5
reg_lambda = 1.0
SHARE = 128
STRETCH = 1024
GROUPS = 4
HIGHS = 8
LOWS = 256 // HIGHS
CHUNK = 256
BLOCK = 512


def node_column(smaller_ref, parents):
    which = lax.broadcasted_iota(jnp.int32, (parents, 1), 0)
    column = jnp.zeros((parents, 1), jnp.int32)
    for p in range(parents):
        column = jnp.where(which == p, smaller_ref[p], column)
    return column


def count_column(counts_ref):
    which = lax.broadcasted_iota(jnp.int32, (8, 1), 0)
    column = jnp.zeros((8, 1), jnp.int32)
    for q in range(counts_ref.shape[0]):
        column = jnp.where(which == q, counts_ref[q], column)
    return column


def lambda_kernel(counts_ref, scores_ref, labels_ref, lam_ref, rows_ref, cols_ref, sums_ref):
    query_dev, slots = scores_ref.shape
    own = pl.multiple_of(lax.axis_index("feat") * SHARE, SHARE)
    position = lax.broadcasted_iota(jnp.int32, (8, slots), 1)
    discount = 1.0 / jnp.log2(position.astype(jnp.float32) + 2.0)
    counts = count_column(counts_ref)
    grade = labels_ref[...]
    usable = position[:query_dev] < counts[:query_dev]
    rows_ref[0:16, :] = jnp.zeros((16, slots), jnp.float32)
    rows_ref[0:query_dev, :] = jnp.where(usable, jnp.exp(scores_ref[...]), 0.0)
    rows_ref[8 : 8 + query_dev, :] = jnp.where(usable, jnp.exp2(grade.astype(jnp.float32)) - 1.0, -1.0)
    rows_ref[16:24, :] = discount
    cols_ref[...] = rows_ref[...].T
    sums_ref[...] = jnp.zeros_like(sums_ref)

    ideal = jnp.zeros((query_dev, slots), jnp.float32)
    ahead = jnp.zeros((query_dev, 1), jnp.int32)
    for c in range(levels - 1, 0, -1):
        here = jnp.sum(((grade == c) & usable).astype(jnp.float32), axis=1, keepdims=True).astype(jnp.int32)
        span = (position[:query_dev] >= ahead) & (position[:query_dev] < ahead + here)
        ideal = ideal + jnp.where(span, float(2**c - 1), 0.0)
        ahead = ahead + here
    ideal = jnp.sum(ideal * discount[:query_dev], axis=1, keepdims=True)
    inv_ideal = 1.0 / jnp.maximum(ideal, 1.0)

    for q in range(query_dev):
        count = counts_ref[q]
        e_i = rows_ref[q : q + 1, pl.ds(own, SHARE)]
        g_i = rows_ref[8 + q : 9 + q, pl.ds(own, SHARE)]
        d_i = rows_ref[16:17, pl.ds(own, SHARE)]

        def partners(jb, sums, q=q, e_i=e_i, g_i=g_i, d_i=d_i):
            grad_sum, hess_sum = sums
            at = pl.ds(pl.multiple_of(jb * STRETCH, STRETCH), STRETCH)
            e_j = cols_ref[at, q : q + 1]
            g_j = cols_ref[at, 8 + q : 9 + q]
            d_j = cols_ref[at, 16:17]
            inverse = 1.0 / (e_i + e_j)
            gain_gap = g_i - g_j
            higher = gain_gap > 0.0
            part = gain_gap * (jnp.abs(d_i - d_j) * inverse)
            grad = part * jnp.where(higher, e_j, e_i)
            hess = jnp.abs(grad) * (inverse * jnp.where(higher, e_i, e_j))
            grad_sum = grad_sum + jnp.sum(grad.reshape(STRETCH // 32, 32, SHARE), axis=0)
            hess_sum = hess_sum + jnp.sum(hess.reshape(STRETCH // 32, 32, SHARE), axis=0)
            return grad_sum, hess_sum

        zero = jnp.zeros((32, SHARE), jnp.float32)
        last = jnp.where(own < count, (count + STRETCH - 1) // STRETCH, 0)
        grad_sum, hess_sum = lax.fori_loop(0, last, partners, (zero, zero))
        sums_ref[q : q + 1, :] = -jnp.sum(grad_sum, axis=0, keepdims=True)
        sums_ref[8 + q : 9 + q, :] = jnp.sum(hess_sum, axis=0, keepdims=True)

    mine = own + lax.broadcasted_iota(jnp.int32, (query_dev, SHARE), 1) < counts[:query_dev]
    sums_ref[0:query_dev, :] = jnp.where(mine, sums_ref[0:query_dev, :] * inv_ideal, 0.0)
    sums_ref[8 : 8 + query_dev, :] = jnp.where(mine, sums_ref[8 : 8 + query_dev, :] * inv_ideal, 0.0)
    lam_ref[...] = jnp.broadcast_to(sums_ref[...].astype(jnp.bfloat16)[None], lam_ref.shape)


def lambdas(scores, labels, counts):
    query_dev, slots = scores.shape
    vmem = pl.BlockSpec(memory_space=pltpu.VMEM)
    smem = pl.BlockSpec(memory_space=pltpu.SMEM)
    return pl.pallas_call(
        lambda_kernel,
        out_shape=jax.ShapeDtypeStruct((slots // SHARE, 16, SHARE), jnp.bfloat16),
        in_specs=[smem, vmem, vmem],
        out_specs=vmem,
        scratch_shapes=[
            pltpu.VMEM((24, slots), jnp.float32),
            pltpu.VMEM((slots, 24), jnp.float32),
            pltpu.VMEM((16, SHARE), jnp.float32),
        ],
        name="lambdas",
    )(counts, scores, labels)


def prefix_lanes(values):
    lane = lax.broadcasted_iota(jnp.int32, values.shape, 1)
    step = 1
    while step < values.shape[1]:
        values = values + jnp.where(lane >= step, pltpu.roll(values, step, 1), 0.0)
        step *= 2
    return values


def compact(
    smaller_ref, counts_ref, lam_ref, child_ref, codes_ref,
    high_ref, low_ref, weight_ref, moved_ref, spot_ref, chunks_ref,
):
    query_dev, feats, slots = codes_ref.shape
    parents = smaller_ref.shape[0]
    per_group = parents // GROUPS
    blocks = slots // BLOCK
    lam = jnp.concatenate([lam_ref[k].astype(jnp.float32) for k in range(lam_ref.shape[0])], axis=1)
    child = child_ref[...]
    parent = child >> 1
    wanted = jnp.zeros_like(child)
    for p in range(parents):
        wanted = jnp.where(parent == p, smaller_ref[p], wanted)
    position = lax.broadcasted_iota(jnp.int32, child.shape, 1)
    usable = position < count_column(counts_ref)[:query_dev]
    live = ((child & 1) == wanted) & usable
    owner = jnp.where(live, parent // per_group, -1)
    numbers = {}
    ranks = []
    for g in range(0, GROUPS, 2):
        pair = jnp.where(owner == g, 1, jnp.where(owner == g + 1, 4096, 0)).astype(jnp.float32)
        for q in range(query_dev):
            for k in range(blocks):
                total = jnp.sum(pair[q : q + 1, k * BLOCK : (k + 1) * BLOCK]).astype(jnp.int32)
                numbers[g, q, k] = total & 4095
                numbers[g + 1, q, k] = total >> 12
        packed = (prefix_lanes(pair) - pair).astype(jnp.int32)
        ranks += [(packed & 4095).astype(jnp.float32), (packed >> 12).astype(jnp.float32)]
    starts = {}
    base = jnp.int32(0)
    crowded = jnp.int32(0)
    which = lax.broadcasted_iota(jnp.int32, (8, 1), 0)
    for g in range(GROUPS):
        first = base
        opening = jnp.zeros((8, 1), jnp.float32)
        for q in range(query_dev):
            opening = jnp.where(which == q, first.astype(jnp.float32), opening)
            for k in range(blocks):
                starts[g, q, k] = first
                first = first + numbers[g, q, k]
                crowded = jnp.maximum(crowded, numbers[g, q, k])
        spot_ref[g, 0:query_dev, :] = jnp.where(owner == g, ranks[g] + opening[:query_dev], -1.0)
        chunks = (first - base + CHUNK - 1) // CHUNK
        chunks_ref[g, 0] = base // CHUNK
        chunks_ref[g, 1] = chunks
        base = base + chunks * CHUNK

    def clear(t, carry):
        at = pl.ds(pl.multiple_of(t * CHUNK, CHUNK), CHUNK)
        low_ref[:, at] = jnp.zeros((feats, CHUNK), jnp.float32)
        weight_ref[:, at] = jnp.zeros((16, CHUNK), jnp.float32)
        return carry

    lax.fori_loop(0, base // CHUNK, clear, 0)
    local = lax.broadcasted_iota(jnp.int32, (per_group, 1), 0)
    for q in range(query_dev):
        member = ((parent[q : q + 1] % per_group) == local) & live[q : q + 1]
        grad = jnp.where(member, lam[q : q + 1], 0.0)
        hess = jnp.where(member, lam[8 + q : 9 + q], 0.0)
        rows = jnp.concatenate((grad, hess) * GROUPS, axis=0)
        moved_ref[q, 0:feats, :] = codes_ref[q].astype(jnp.float32).astype(jnp.bfloat16)
        moved_ref[q, feats : feats + 16, :] = rows.astype(jnp.bfloat16)
    mark = lax.broadcasted_iota(jnp.int32, (128, 1), 0).astype(jnp.float32)
    lane = lax.broadcasted_iota(jnp.int32, (1, 128), 1)
    one = jnp.ones((), jnp.bfloat16)
    zero = jnp.zeros((), jnp.bfloat16)

    def place(skip):
        for q in range(query_dev):
            for k in range(blocks):
                block = slice(k * BLOCK, (k + 1) * BLOCK)
                moved = moved_ref[q, :, block]
                for g in range(GROUPS):
                    begin = starts[g, q, k]
                    to = pl.multiple_of((begin // 128) * 128, 128)
                    offset = begin - to
                    ahead = spot_ref[g, q : q + 1, block] - (to + skip).astype(jnp.float32)
                    shift = offset.astype(jnp.float32)
                    here = jnp.where((ahead >= shift) & (ahead < shift + 128.0), ahead, -1.0)
                    here = jnp.where(here >= 128.0, here - 128.0, here)
                    hot = jnp.where(here == mark, one, zero)
                    out = lax.dot_general(
                        moved, hot, (((1,), (1,)), ((), ())), preferred_element_type=jnp.float32
                    )
                    now = jnp.where(lane >= offset, out, 0.0)
                    then = jnp.where(lane >= offset, 0.0, out)
                    for add, start in ((now, to + skip), (then, to + skip + 128)):
                        at = pl.ds(pl.multiple_of(start, 128), 128)
                        low_ref[:, at] += add[:feats]
                        weight_ref[:, at] += add[feats:]

    def turn(t, carry):
        place(t * 128)
        return carry

    lax.fori_loop(0, (crowded + 127) // 128, turn, 0)

    def split(t, carry):
        at = pl.ds(pl.multiple_of(t * CHUNK, CHUNK), CHUNK)
        code = low_ref[:, at]
        high = jnp.floor(code * (1.0 / LOWS))
        high_ref[:, at] = high
        low_ref[:, at] = code - high * LOWS
        return carry

    lax.fori_loop(0, base // CHUNK, split, 0)


def histogram_kernel(
    smaller_ref, counts_ref, lam_ref, child_ref, codes_ref, hist_ref,
    high_ref, low_ref, weight_ref, moved_ref, spot_ref, acc_ref, chunks_ref,
):
    feats = hist_ref.shape[0]
    compact(
        smaller_ref, counts_ref, lam_ref, child_ref, codes_ref,
        high_ref, low_ref, weight_ref, moved_ref, spot_ref, chunks_ref,
    )
    kinds = 16 // GROUPS
    wide = HIGHS * kinds
    one = jnp.ones((), jnp.bfloat16)
    zero = jnp.zeros((), jnp.bfloat16)
    low_mark = lax.broadcasted_iota(jnp.int32, (LOWS, 1), 0).astype(jnp.float32).astype(jnp.bfloat16)
    slot = lax.broadcasted_iota(jnp.int32, (16, 1), 0) // kinds
    lane = lax.broadcasted_iota(jnp.int32, (1, 128), 1)
    acc_ref[...] = jnp.zeros_like(acc_ref)
    for g in range(GROUPS):

        def chunk(t, carry, g=g, size=CHUNK):
            at = pl.ds(pl.multiple_of((chunks_ref[g, 0] + t) * CHUNK, CHUNK), size)
            weight = weight_ref[:, at].astype(jnp.bfloat16)
            for first in range(0, feats, HIGHS):
                lhs = []
                rhs = [None] * HIGHS
                for k in range(HIGHS):
                    f = first + k
                    high = jnp.broadcast_to(high_ref[f : f + 1, at], (16, size)).astype(jnp.bfloat16)
                    low = jnp.broadcast_to(low_ref[f : f + 1, at], (LOWS, size)).astype(jnp.bfloat16)
                    for j in range(wide // 16):
                        marks = (slot + j * GROUPS).astype(jnp.float32).astype(jnp.bfloat16)
                        lhs.append(jnp.where(high == marks, weight, zero))
                    rhs[k // GROUPS * GROUPS + (k + g) % GROUPS] = jnp.where(low == low_mark, one, zero)
                out = lax.dot_general(
                    jnp.concatenate(lhs, axis=0), jnp.concatenate(rhs, axis=0),
                    (((1,), (1,)), ((), ())), preferred_element_type=jnp.float32,
                )
                for k in range(HIGHS):
                    half = k // GROUPS * 128
                    mine = lane // LOWS == (k + g) % GROUPS
                    acc_ref[first + k] += jnp.where(
                        mine, out[k * wide : (k + 1) * wide, half : half + 128], 0.0
                    )
            return carry

        def double(t, carry, chunk=chunk):
            return chunk(2 * t, carry, size=2 * CHUNK)

        pairs = chunks_ref[g, 1] // 2
        lax.fori_loop(0, pairs, double, 0)
        lax.fori_loop(2 * pairs, chunks_ref[g, 1], chunk, 0)
    hist_ref[...] = acc_ref[...].astype(jnp.bfloat16)


def histograms(smaller, counts, lam, row_child, bin_codes):
    query_dev, feat_dev, slots = bin_codes.shape
    room = query_dev * slots + GROUPS * CHUNK + BLOCK + 256
    vmem = pl.BlockSpec(memory_space=pltpu.VMEM)
    smem = pl.BlockSpec(memory_space=pltpu.SMEM)
    wide = HIGHS * 16 // GROUPS
    return pl.pallas_call(
        histogram_kernel,
        out_shape=jax.ShapeDtypeStruct((feat_dev, wide, 128), jnp.bfloat16),
        in_specs=[smem, smem, vmem, vmem, vmem],
        out_specs=vmem,
        scratch_shapes=[
            pltpu.VMEM((feat_dev, room), jnp.float32),
            pltpu.VMEM((feat_dev, room), jnp.float32),
            pltpu.VMEM((16, room), jnp.float32),
            pltpu.VMEM((query_dev, feat_dev + 16, slots), jnp.bfloat16),
            pltpu.VMEM((GROUPS, 8, slots), jnp.float32),
            pltpu.VMEM((feat_dev, wide, 128), jnp.float32),
            pltpu.SMEM((GROUPS, 2), jnp.int32),
        ],
        name="histograms",
    )(smaller, counts, lam, row_child, bin_codes)


def gain_kernel(parts_ref, send_ref):
    wide = HIGHS * 16 // GROUPS
    feats = parts_ref.shape[1] // wide
    bins = HIGHS * LOWS
    kinds = 16 // GROUPS
    summed = jnp.sum(parts_ref[...].astype(jnp.float32), axis=0)
    built = []
    for f in range(feats):
        turn = (lax.axis_index("row") * feats + f) % GROUPS
        block = pltpu.roll(summed[f * wide : (f + 1) * wide], (GROUPS - turn) * LOWS % 128, 1)
        stats = ([], [])
        for g in range(GROUPS):
            pieces = [block[h * kinds : (h + 1) * kinds, g * LOWS : (g + 1) * LOWS] for h in range(HIGHS)]
            both = jnp.concatenate(pieces, axis=1)
            stats[0].append(both[: kinds // 2])
            stats[1].append(both[kinds // 2 :])
        built += stats[0] + stats[1]
    built = jnp.concatenate(built, axis=0)
    rows = built.shape[0]
    below = lax.broadcasted_iota(jnp.int32, (bins, bins), 0)
    upto = lax.broadcasted_iota(jnp.int32, (bins, bins), 1)
    left = jnp.dot(
        built, (below <= upto).astype(jnp.float32),
        precision=lax.Precision.HIGHEST, preferred_element_type=jnp.float32,
    )
    threshold = lax.broadcasted_iota(jnp.int32, (8, bins), 1)
    best = jnp.full((8, 1), -jnp.inf, jnp.float32)
    for f in range(feats):
        grad_left = left[f * 16 : f * 16 + 8]
        hess_left = left[f * 16 + 8 : f * 16 + 16]
        grad_total = grad_left[:, bins - 1 : bins]
        hess_total = hess_left[:, bins - 1 : bins]
        grad_right = grad_total - grad_left
        gain = (
            grad_left * grad_left / (hess_left + reg_lambda)
            + grad_right * grad_right / (hess_total - hess_left + reg_lambda)
            - grad_total * grad_total / (hess_total + reg_lambda)
        )
        gain = jnp.where(threshold < bins - 1, gain, -jnp.inf)
        best = jnp.maximum(best, jnp.max(gain, axis=1, keepdims=True))
    stacked = jnp.concatenate(
        (built, jnp.broadcast_to(best, (8, bins)), jnp.zeros((128 - rows - 8, bins), jnp.float32)), axis=0
    )
    by_bin = stacked.T.reshape(send_ref.shape[0], -1, 128)
    half = send_ref.shape[1]
    send_ref[...] = jnp.concatenate((by_bin[:, :half, :64], by_bin[:, half:, :64]), axis=2)


def children_kernel(smaller_ref, parts_ref, parent_ref, children_ref):
    sources, half, lanes = parts_ref.shape
    bin_span, parents, width = children_ref.shape
    group = width // sources
    column = lax.broadcasted_iota(jnp.int32, (sources, width), 1)
    source = lax.broadcasted_iota(jnp.int32, (sources, width), 0)
    spread = (column // group == source).astype(jnp.float32)
    rows = group * parents // 2
    row = lax.broadcasted_iota(jnp.int32, (rows, width), 0)
    col = lax.broadcasted_iota(jnp.int32, (rows, width), 1)
    match = (row // (2 * parents) == (col % group) // 4) & ((row // parents) % 2 == col % 2)
    pick_row = lax.broadcasted_iota(jnp.int32, (width // 2, width), 0)
    pick_col = lax.broadcasted_iota(jnp.int32, (width // 2, width), 1)
    pick = (pick_row == (pick_col // 4) * 2 + pick_col % 2).astype(jnp.float32)
    side = (lax.broadcasted_iota(jnp.int32, (parents, width), 1) // 2) % 2
    chosen = side == node_column(smaller_ref, parents)
    parent = jnp.dot(
        parent_ref[...].reshape(bin_span * parents, width // 2), pick,
        precision=lax.Precision.HIGHEST, preferred_element_type=jnp.float32,
    )
    for b in range(bin_span):
        if b < half:
            wide = lax.dot_general(
                parts_ref[:, b, :], spread, (((0,), (0,)), ((), ())),
                precision=lax.Precision.HIGHEST, preferred_element_type=jnp.float32,
            )
            later = (wide[64 : 64 + rows],) if b == 0 else later + (wide[64 : 64 + rows],)
            kept = jnp.where(match, wide[:rows], 0.0)
        else:
            kept = jnp.where(match, later[b - half], 0.0)
        built = jnp.sum(kept.reshape(rows // parents, parents, width), axis=0)
        children_ref[b] = jnp.where(chosen, built, parent[b * parents : (b + 1) * parents] - built)


def shards(scores, labels, counts, bin_codes, row_child, smaller, parent_hist):
    feat_dev = bin_codes.shape[1]
    bin_span, parents, _ = parent_hist.shape
    row_count = lax.axis_size("row")
    feat_count = lax.axis_size("feat")
    rows = feat_dev // row_count * 2 * parents
    bins = bin_span * row_count
    vmem = pl.BlockSpec(memory_space=pltpu.VMEM)
    smem = pl.BlockSpec(memory_space=pltpu.SMEM)
    lam = lax.all_to_all(lambdas(scores, labels, counts), "feat", 0, 0, tiled=True)
    hist = histograms(smaller, counts, lam, row_child, bin_codes)
    parts = lax.all_to_all(hist.reshape(row_count, -1, 128), "row", 0, 0, tiled=True)
    send = pl.pallas_call(
        gain_kernel,
        out_shape=jax.ShapeDtypeStruct((row_count, bin_span // 2, 128), jnp.float32),
        in_specs=[vmem], out_specs=vmem, name="gains",
    )(parts)
    own = lax.all_to_all(send, "row", 0, 0, tiled=True)
    best = jnp.broadcast_to(jnp.max(own, axis=0)[None], (feat_count, bin_span // 2, 128))
    best = jnp.max(lax.all_to_all(best, "feat", 0, 0, tiled=True), axis=0)
    children = pl.pallas_call(
        children_kernel,
        out_shape=jax.ShapeDtypeStruct((bin_span, parents, feat_dev * 4), jnp.float32),
        in_specs=[smem, vmem, vmem], out_specs=vmem, name="children",
    )(smaller, own, parent_hist)
    return children, best[0, rows : rows + parents]


def solution(mesh):
    placed = (
        P("row", None), P("row", None), P("row"), P("row", "feat", None),
        P("row", None), P(), P("row", None, "feat"),
    )
    return jax.shard_map(
        shards, mesh=mesh, in_specs=placed, out_specs=(P("row", None, "feat"), P()), check_vma=False
    )
```

```python
import jax
import jax.numpy as jnp
from jax import lax
from jax.experimental import pallas as pl
from jax.experimental.pallas import tpu as pltpu
from jax.sharding import PartitionSpec as P

levels = 5
reg_lambda = 1.0
SHARE = 128
STRETCH = 1024
GROUPS = 4
HIGHS = 8
LOWS = 256 // HIGHS
CHUNK = 256
BLOCK = 512
INNER = 8


def node_column(smaller_ref, parents):
    which = lax.broadcasted_iota(jnp.int32, (parents, 1), 0)
    column = jnp.zeros((parents, 1), jnp.int32)
    for p in range(parents):
        column = jnp.where(which == p, smaller_ref[p], column)
    return column


def count_column(counts_ref):
    which = lax.broadcasted_iota(jnp.int32, (8, 1), 0)
    column = jnp.zeros((8, 1), jnp.int32)
    for q in range(counts_ref.shape[0]):
        column = jnp.where(which == q, counts_ref[q], column)
    return column


def lambda_kernel(counts_ref, scores_ref, labels_ref, lam_ref, rows_ref, cols_ref, sums_ref):
    query_dev, slots = scores_ref.shape
    own = pl.multiple_of(lax.axis_index("feat") * SHARE, SHARE)
    position = lax.broadcasted_iota(jnp.int32, (8, slots), 1)
    discount = 1.0 / jnp.log2(position.astype(jnp.float32) + 2.0)
    counts = count_column(counts_ref)
    grade = labels_ref[...]
    usable = position[:query_dev] < counts[:query_dev]
    rows_ref[0:16, :] = jnp.zeros((16, slots), jnp.float32)
    rows_ref[0:query_dev, :] = jnp.where(usable, jnp.exp(scores_ref[...]), 0.0)
    rows_ref[8 : 8 + query_dev, :] = jnp.where(usable, jnp.exp2(grade.astype(jnp.float32)) - 1.0, -1.0)
    rows_ref[16:24, :] = discount
    cols_ref[...] = rows_ref[...].T
    sums_ref[...] = jnp.zeros_like(sums_ref)

    ideal = jnp.zeros((query_dev, slots), jnp.float32)
    ahead = jnp.zeros((query_dev, 1), jnp.int32)
    for c in range(levels - 1, 0, -1):
        here = jnp.sum(((grade == c) & usable).astype(jnp.float32), axis=1, keepdims=True).astype(jnp.int32)
        span = (position[:query_dev] >= ahead) & (position[:query_dev] < ahead + here)
        ideal = ideal + jnp.where(span, float(2**c - 1), 0.0)
        ahead = ahead + here
    ideal = jnp.sum(ideal * discount[:query_dev], axis=1, keepdims=True)
    inv_ideal = 1.0 / jnp.maximum(ideal, 1.0)

    for q in range(query_dev):
        count = counts_ref[q]
        e_i = rows_ref[q : q + 1, pl.ds(own, SHARE)]
        g_i = rows_ref[8 + q : 9 + q, pl.ds(own, SHARE)]
        d_i = rows_ref[16:17, pl.ds(own, SHARE)]

        def partners(jb, sums, q=q, e_i=e_i, g_i=g_i, d_i=d_i):
            grad_sum, hess_sum = sums
            at = pl.ds(pl.multiple_of(jb * STRETCH, STRETCH), STRETCH)
            e_j = cols_ref[at, q : q + 1]
            g_j = cols_ref[at, 8 + q : 9 + q]
            d_j = cols_ref[at, 16:17]
            inverse = 1.0 / (e_i + e_j)
            gain_gap = g_i - g_j
            higher = gain_gap > 0.0
            part = gain_gap * (jnp.abs(d_i - d_j) * inverse)
            grad = part * jnp.where(higher, e_j, e_i)
            hess = jnp.abs(grad) * (inverse * jnp.where(higher, e_i, e_j))
            grad_sum = grad_sum + jnp.sum(grad.reshape(STRETCH // 32, 32, SHARE), axis=0)
            hess_sum = hess_sum + jnp.sum(hess.reshape(STRETCH // 32, 32, SHARE), axis=0)
            return grad_sum, hess_sum

        zero = jnp.zeros((32, SHARE), jnp.float32)
        last = jnp.where(own < count, (count + STRETCH - 1) // STRETCH, 0)
        grad_sum, hess_sum = lax.fori_loop(0, last, partners, (zero, zero))
        sums_ref[q : q + 1, :] = -jnp.sum(grad_sum, axis=0, keepdims=True)
        sums_ref[8 + q : 9 + q, :] = jnp.sum(hess_sum, axis=0, keepdims=True)

    mine = own + lax.broadcasted_iota(jnp.int32, (query_dev, SHARE), 1) < counts[:query_dev]
    sums_ref[0:query_dev, :] = jnp.where(mine, sums_ref[0:query_dev, :] * inv_ideal, 0.0)
    sums_ref[8 : 8 + query_dev, :] = jnp.where(mine, sums_ref[8 : 8 + query_dev, :] * inv_ideal, 0.0)
    lam_ref[...] = jnp.broadcast_to(sums_ref[...].astype(jnp.bfloat16)[None], lam_ref.shape)


def lambdas(scores, labels, counts):
    query_dev, slots = scores.shape
    vmem = pl.BlockSpec(memory_space=pltpu.VMEM)
    smem = pl.BlockSpec(memory_space=pltpu.SMEM)
    return pl.pallas_call(
        lambda_kernel,
        out_shape=jax.ShapeDtypeStruct((slots // SHARE, 16, SHARE), jnp.bfloat16),
        in_specs=[smem, vmem, vmem],
        out_specs=vmem,
        scratch_shapes=[
            pltpu.VMEM((24, slots), jnp.float32),
            pltpu.VMEM((slots, 24), jnp.float32),
            pltpu.VMEM((16, SHARE), jnp.float32),
        ],
        name="lambdas",
    )(counts, scores, labels)


def prefix_lanes(values):
    lane = lax.broadcasted_iota(jnp.int32, values.shape, 1)
    step = 1
    while step < values.shape[1]:
        values = values + jnp.where(lane >= step, pltpu.roll(values, step, 1), 0.0)
        step *= 2
    return values


def compact(
    smaller_ref, counts_ref, lam_ref, child_ref, codes_ref,
    high_ref, low_ref, weight_ref, moved_ref, spot_ref, chunks_ref,
):
    query_dev, feats, slots = codes_ref.shape
    parents = smaller_ref.shape[0]
    per_group = parents // GROUPS
    blocks = slots // BLOCK
    lam = jnp.concatenate([lam_ref[k].astype(jnp.float32) for k in range(lam_ref.shape[0])], axis=1)
    child = child_ref[...]
    parent = child >> 1
    wanted = jnp.zeros_like(child)
    for p in range(parents):
        wanted = jnp.where(parent == p, smaller_ref[p], wanted)
    position = lax.broadcasted_iota(jnp.int32, child.shape, 1)
    usable = position < count_column(counts_ref)[:query_dev]
    live = ((child & 1) == wanted) & usable
    owner = jnp.where(live, parent // per_group, -1)
    numbers = {}
    ranks = []
    for g in range(0, GROUPS, 2):
        pair = jnp.where(owner == g, 1, jnp.where(owner == g + 1, 4096, 0)).astype(jnp.float32)
        for q in range(query_dev):
            for k in range(blocks):
                total = jnp.sum(pair[q : q + 1, k * BLOCK : (k + 1) * BLOCK]).astype(jnp.int32)
                numbers[g, q, k] = total & 4095
                numbers[g + 1, q, k] = total >> 12
        packed = (prefix_lanes(pair) - pair).astype(jnp.int32)
        ranks += [(packed & 4095).astype(jnp.float32), (packed >> 12).astype(jnp.float32)]
    starts = {}
    base = jnp.int32(0)
    crowded = jnp.int32(0)
    which = lax.broadcasted_iota(jnp.int32, (8, 1), 0)
    for g in range(GROUPS):
        first = base
        opening = jnp.zeros((8, 1), jnp.float32)
        for q in range(query_dev):
            opening = jnp.where(which == q, first.astype(jnp.float32), opening)
            for k in range(blocks):
                starts[g, q, k] = first
                first = first + numbers[g, q, k]
                crowded = jnp.maximum(crowded, numbers[g, q, k])
        spot_ref[g, 0:query_dev, :] = jnp.where(owner == g, ranks[g] + opening[:query_dev], -1.0)
        chunks = (first - base + CHUNK - 1) // CHUNK
        chunks_ref[g, 0] = base // CHUNK
        chunks_ref[g, 1] = chunks
        base = base + chunks * CHUNK

    def clear(t, carry):
        at = pl.ds(pl.multiple_of(t * CHUNK, CHUNK), CHUNK)
        low_ref[:, at] = jnp.zeros((feats, CHUNK), jnp.float32)
        weight_ref[:, at] = jnp.zeros((16, CHUNK), jnp.float32)
        return carry

    lax.fori_loop(0, base // CHUNK, clear, 0)
    local = lax.broadcasted_iota(jnp.int32, (per_group, 1), 0)
    for q in range(query_dev):
        member = ((parent[q : q + 1] % per_group) == local) & live[q : q + 1]
        grad = jnp.where(member, lam[q : q + 1], 0.0)
        hess = jnp.where(member, lam[8 + q : 9 + q], 0.0)
        rows = jnp.concatenate((grad, hess) * GROUPS, axis=0)
        moved_ref[q, 0:feats, :] = codes_ref[q].astype(jnp.float32).astype(jnp.bfloat16)
        moved_ref[q, feats : feats + 16, :] = rows.astype(jnp.bfloat16)
    mark = lax.broadcasted_iota(jnp.int32, (128, 1), 0).astype(jnp.float32)
    lane = lax.broadcasted_iota(jnp.int32, (1, 128), 1)
    one = jnp.ones((), jnp.bfloat16)
    zero = jnp.zeros((), jnp.bfloat16)

    def place(skip):
        for q in range(query_dev):
            for k in range(blocks):
                block = slice(k * BLOCK, (k + 1) * BLOCK)
                moved = moved_ref[q, :, block]
                for g in range(GROUPS):
                    begin = starts[g, q, k]
                    to = pl.multiple_of((begin // 128) * 128, 128)
                    offset = begin - to
                    ahead = spot_ref[g, q : q + 1, block] - (to + skip).astype(jnp.float32)
                    shift = offset.astype(jnp.float32)
                    here = jnp.where((ahead >= shift) & (ahead < shift + 128.0), ahead, -1.0)
                    here = jnp.where(here >= 128.0, here - 128.0, here)
                    hot = jnp.where(here == mark, one, zero)
                    out = lax.dot_general(
                        moved, hot, (((1,), (1,)), ((), ())), preferred_element_type=jnp.float32
                    )
                    now = jnp.where(lane >= offset, out, 0.0)
                    then = jnp.where(lane >= offset, 0.0, out)
                    for add, start in ((now, to + skip), (then, to + skip + 128)):
                        at = pl.ds(pl.multiple_of(start, 128), 128)
                        low_ref[:, at] += add[:feats]
                        weight_ref[:, at] += add[feats:]

    def turn(t, carry):
        place(t * 128)
        return carry

    lax.fori_loop(0, (crowded + 127) // 128, turn, 0)

    def split(t, carry):
        at = pl.ds(pl.multiple_of(t * CHUNK, CHUNK), CHUNK)
        code = low_ref[:, at]
        high = jnp.floor(code * (1.0 / LOWS))
        high_ref[:, at] = high
        low_ref[:, at] = code - high * LOWS
        return carry

    lax.fori_loop(0, base // CHUNK, split, 0)


def histogram_kernel(
    smaller_ref, counts_ref, lam_ref, child_ref, codes_ref, hist_ref,
    high_ref, low_ref, weight_ref, moved_ref, spot_ref, acc_ref, chunks_ref,
):
    feats = hist_ref.shape[0]
    compact(
        smaller_ref, counts_ref, lam_ref, child_ref, codes_ref,
        high_ref, low_ref, weight_ref, moved_ref, spot_ref, chunks_ref,
    )
    kinds = 16 // GROUPS
    wide = HIGHS * kinds
    one = jnp.ones((), jnp.bfloat16)
    zero = jnp.zeros((), jnp.bfloat16)
    low_mark = lax.broadcasted_iota(jnp.int32, (LOWS, 1), 0).astype(jnp.float32).astype(jnp.bfloat16)
    slot = lax.broadcasted_iota(jnp.int32, (16, 1), 0) // kinds
    lane = lax.broadcasted_iota(jnp.int32, (1, 128), 1)
    acc_ref[...] = jnp.zeros_like(acc_ref)
    for g in range(GROUPS):

        def chunk(t, carry, g=g, size=CHUNK):
            at = pl.ds(pl.multiple_of((chunks_ref[g, 0] + t) * CHUNK, CHUNK), size)
            weight = weight_ref[:, at].astype(jnp.bfloat16)
            for first in range(0, feats, HIGHS):
                lhs = []
                rhs = [None] * HIGHS
                for k in range(HIGHS):
                    f = first + k
                    high = jnp.broadcast_to(high_ref[f : f + 1, at], (16, size)).astype(jnp.bfloat16)
                    low = jnp.broadcast_to(low_ref[f : f + 1, at], (LOWS, size)).astype(jnp.bfloat16)
                    for j in range(wide // 16):
                        marks = (slot + j * GROUPS).astype(jnp.float32).astype(jnp.bfloat16)
                        lhs.append(jnp.where(high == marks, weight, zero))
                    rhs[k // GROUPS * GROUPS + (k + g) % GROUPS] = jnp.where(low == low_mark, one, zero)
                out = lax.dot_general(
                    jnp.concatenate(lhs, axis=0), jnp.concatenate(rhs, axis=0),
                    (((1,), (1,)), ((), ())), preferred_element_type=jnp.float32,
                )
                for k in range(HIGHS):
                    half = k // GROUPS * 128
                    mine = lane // LOWS == (k + g) % GROUPS
                    acc_ref[first + k] += jnp.where(
                        mine, out[k * wide : (k + 1) * wide, half : half + 128], 0.0
                    )
            return carry

        def double(t, carry, chunk=chunk):
            return chunk(2 * t, carry, size=2 * CHUNK)

        pairs = chunks_ref[g, 1] // 2
        lax.fori_loop(0, pairs, double, 0)
        lax.fori_loop(2 * pairs, chunks_ref[g, 1], chunk, 0)
    hist_ref[...] = acc_ref[...].astype(jnp.bfloat16)


def histograms(smaller, counts, lam, row_child, bin_codes):
    query_dev, feat_dev, slots = bin_codes.shape
    room = query_dev * slots + GROUPS * CHUNK + BLOCK + 256
    vmem = pl.BlockSpec(memory_space=pltpu.VMEM)
    smem = pl.BlockSpec(memory_space=pltpu.SMEM)
    wide = HIGHS * 16 // GROUPS
    return pl.pallas_call(
        histogram_kernel,
        out_shape=jax.ShapeDtypeStruct((feat_dev, wide, 128), jnp.bfloat16),
        in_specs=[smem, smem, vmem, vmem, vmem],
        out_specs=vmem,
        scratch_shapes=[
            pltpu.VMEM((feat_dev, room), jnp.float32),
            pltpu.VMEM((feat_dev, room), jnp.float32),
            pltpu.VMEM((16, room), jnp.float32),
            pltpu.VMEM((query_dev, feat_dev + 16, slots), jnp.bfloat16),
            pltpu.VMEM((GROUPS, 8, slots), jnp.float32),
            pltpu.VMEM((feat_dev, wide, 128), jnp.float32),
            pltpu.SMEM((GROUPS, 2), jnp.int32),
        ],
        name="histograms",
    )(smaller, counts, lam, row_child, bin_codes)


def gain_kernel(parts_ref, send_ref):
    wide = HIGHS * 16 // GROUPS
    feats = parts_ref.shape[1] // wide
    bins = HIGHS * LOWS
    kinds = 16 // GROUPS
    summed = jnp.sum(parts_ref[...].astype(jnp.float32), axis=0)
    built = []
    for f in range(feats):
        turn = (lax.axis_index("row") * feats + f) % GROUPS
        block = pltpu.roll(summed[f * wide : (f + 1) * wide], (GROUPS - turn) * LOWS % 128, 1)
        stats = ([], [])
        for g in range(GROUPS):
            pieces = [block[h * kinds : (h + 1) * kinds, g * LOWS : (g + 1) * LOWS] for h in range(HIGHS)]
            both = jnp.concatenate(pieces, axis=1)
            stats[0].append(both[: kinds // 2])
            stats[1].append(both[kinds // 2 :])
        built += stats[0] + stats[1]
    built = jnp.concatenate(built, axis=0)
    rows = built.shape[0]
    below = lax.broadcasted_iota(jnp.int32, (bins, bins), 0)
    upto = lax.broadcasted_iota(jnp.int32, (bins, bins), 1)
    left = jnp.dot(
        built, (below <= upto).astype(jnp.float32),
        precision=lax.Precision.HIGHEST, preferred_element_type=jnp.float32,
    )
    threshold = lax.broadcasted_iota(jnp.int32, (8, bins), 1)
    best = jnp.full((8, 1), -jnp.inf, jnp.float32)
    for f in range(feats):
        grad_left = left[f * 16 : f * 16 + 8]
        hess_left = left[f * 16 + 8 : f * 16 + 16]
        grad_total = grad_left[:, bins - 1 : bins]
        hess_total = hess_left[:, bins - 1 : bins]
        grad_right = grad_total - grad_left
        gain = (
            grad_left * grad_left / (hess_left + reg_lambda)
            + grad_right * grad_right / (hess_total - hess_left + reg_lambda)
            - grad_total * grad_total / (hess_total + reg_lambda)
        )
        gain = jnp.where(threshold < bins - 1, gain, -jnp.inf)
        best = jnp.maximum(best, jnp.max(gain, axis=1, keepdims=True))
    stacked = jnp.concatenate(
        (built, jnp.broadcast_to(best, (8, bins)), jnp.zeros((128 - rows - 8, bins), jnp.float32)), axis=0
    )
    by_bin = stacked.T.reshape(send_ref.shape[0], -1, 128)
    half = send_ref.shape[1]
    send_ref[...] = jnp.concatenate((by_bin[:, :half, :64], by_bin[:, half:, :64]), axis=2)


def children_kernel(smaller_ref, parts_ref, parent_ref, children_ref):
    sources, half, lanes = parts_ref.shape
    bin_span, parents, width = children_ref.shape
    group = width // sources
    column = lax.broadcasted_iota(jnp.int32, (sources, width), 1)
    source = lax.broadcasted_iota(jnp.int32, (sources, width), 0)
    spread = (column // group == source).astype(jnp.float32)
    rows = group * parents // 2
    row = lax.broadcasted_iota(jnp.int32, (rows, width), 0)
    col = lax.broadcasted_iota(jnp.int32, (rows, width), 1)
    match = (row // (2 * parents) == (col % group) // 4) & ((row // parents) % 2 == col % 2)
    pick_row = lax.broadcasted_iota(jnp.int32, (width // 2, width), 0)
    pick_col = lax.broadcasted_iota(jnp.int32, (width // 2, width), 1)
    pick = (pick_row == (pick_col // 4) * 2 + pick_col % 2).astype(jnp.float32)
    side = (lax.broadcasted_iota(jnp.int32, (parents, width), 1) // 2) % 2
    chosen = side == node_column(smaller_ref, parents)
    parent = jnp.dot(
        parent_ref[...].reshape(bin_span * parents, width // 2), pick,
        precision=lax.Precision.HIGHEST, preferred_element_type=jnp.float32,
    )
    for b in range(bin_span):
        if b < half:
            wide = lax.dot_general(
                parts_ref[:, b, :], spread, (((0,), (0,)), ((), ())),
                precision=lax.Precision.HIGHEST, preferred_element_type=jnp.float32,
            )
            later = (wide[64 : 64 + rows],) if b == 0 else later + (wide[64 : 64 + rows],)
            kept = jnp.where(match, wide[:rows], 0.0)
        else:
            kept = jnp.where(match, later[b - half], 0.0)
        built = jnp.sum(kept.reshape(rows // parents, parents, width), axis=0)
        children_ref[b] = jnp.where(chosen, built, parent[b * parents : (b + 1) * parents] - built)


def shards(scores, labels, counts, bin_codes, row_child, smaller, parent_hist):
    feat_dev = bin_codes.shape[1]
    bin_span, parents, _ = parent_hist.shape
    row_count = lax.axis_size("row")
    feat_count = lax.axis_size("feat")
    rows = feat_dev // row_count * 2 * parents
    bins = bin_span * row_count
    vmem = pl.BlockSpec(memory_space=pltpu.VMEM)
    smem = pl.BlockSpec(memory_space=pltpu.SMEM)
    lam = lax.all_to_all(lambdas(scores, labels, counts), "feat", 0, 0, tiled=True)
    hist = histograms(smaller, counts, lam, row_child, bin_codes)
    outer = row_count // INNER
    across = [[x * INNER + z for x in range(outer)] for z in range(INNER)]
    along = [[x * INNER + z for z in range(INNER)] for x in range(outer)]
    parts = lax.all_to_all(
        hist.reshape(outer, -1, 128), "row", 0, 0, axis_index_groups=across, tiled=True
    )
    parts = jnp.sum(parts.astype(jnp.float32), axis=0).astype(jnp.bfloat16)
    parts = lax.all_to_all(
        parts.reshape(INNER, -1, 128), "row", 0, 0, axis_index_groups=along, tiled=True
    )
    send = pl.pallas_call(
        gain_kernel,
        out_shape=jax.ShapeDtypeStruct((row_count, bin_span // 2, 128), jnp.float32),
        in_specs=[vmem], out_specs=vmem, name="gains",
    )(parts)
    own = lax.all_to_all(send, "row", 0, 0, tiled=True)
    best = jnp.broadcast_to(jnp.max(own, axis=0)[None], (feat_count, bin_span // 2, 128))
    best = jnp.max(lax.all_to_all(best, "feat", 0, 0, tiled=True), axis=0)
    children = pl.pallas_call(
        children_kernel,
        out_shape=jax.ShapeDtypeStruct((bin_span, parents, feat_dev * 4), jnp.float32),
        in_specs=[smem, vmem, vmem], out_specs=vmem, name="children",
    )(smaller, own, parent_hist)
    return children, best[0, rows : rows + parents]


def solution(mesh):
    placed = (
        P("row", None), P("row", None), P("row"), P("row", "feat", None),
        P("row", None), P(), P("row", None, "feat"),
    )
    return jax.shard_map(
        shards, mesh=mesh, in_specs=placed, out_specs=(P("row", None, "feat"), P()), check_vma=False
    )
```

```python
import jax
import jax.numpy as jnp
from jax import lax
from jax.experimental import pallas as pl
from jax.experimental.pallas import tpu as pltpu
from jax.sharding import PartitionSpec as P

levels = 5
reg_lambda = 1.0
SHARE = 128
STRETCH = 1024
GROUPS = 4
HIGHS = 8
LOWS = 256 // HIGHS
CHUNK = 256
BLOCK = 512
INNER = 8


def node_column(smaller_ref, parents):
    which = lax.broadcasted_iota(jnp.int32, (parents, 1), 0)
    column = jnp.zeros((parents, 1), jnp.int32)
    for p in range(parents):
        column = jnp.where(which == p, smaller_ref[p], column)
    return column


def count_column(counts_ref):
    which = lax.broadcasted_iota(jnp.int32, (8, 1), 0)
    column = jnp.zeros((8, 1), jnp.int32)
    for q in range(counts_ref.shape[0]):
        column = jnp.where(which == q, counts_ref[q], column)
    return column


def lambda_kernel(counts_ref, scores_ref, labels_ref, lam_ref, rows_ref, cols_ref, sums_ref):
    query_dev, slots = scores_ref.shape
    own = pl.multiple_of(lax.axis_index("feat") * SHARE, SHARE)
    position = lax.broadcasted_iota(jnp.int32, (8, slots), 1)
    discount = 1.0 / jnp.log2(position.astype(jnp.float32) + 2.0)
    counts = count_column(counts_ref)
    grade = labels_ref[...]
    usable = position[:query_dev] < counts[:query_dev]
    rows_ref[0:16, :] = jnp.zeros((16, slots), jnp.float32)
    rows_ref[0:query_dev, :] = jnp.where(usable, jnp.exp(scores_ref[...]), 0.0)
    rows_ref[8 : 8 + query_dev, :] = jnp.where(usable, jnp.exp2(grade.astype(jnp.float32)) - 1.0, -1.0)
    rows_ref[16:24, :] = discount
    cols_ref[...] = rows_ref[...].T
    sums_ref[...] = jnp.zeros_like(sums_ref)

    ideal = jnp.zeros((query_dev, slots), jnp.float32)
    ahead = jnp.zeros((query_dev, 1), jnp.int32)
    for c in range(levels - 1, 0, -1):
        here = jnp.sum(((grade == c) & usable).astype(jnp.float32), axis=1, keepdims=True).astype(jnp.int32)
        span = (position[:query_dev] >= ahead) & (position[:query_dev] < ahead + here)
        ideal = ideal + jnp.where(span, float(2**c - 1), 0.0)
        ahead = ahead + here
    ideal = jnp.sum(ideal * discount[:query_dev], axis=1, keepdims=True)
    inv_ideal = 1.0 / jnp.maximum(ideal, 1.0)

    for q in range(query_dev):
        count = counts_ref[q]
        e_i = rows_ref[q : q + 1, pl.ds(own, SHARE)]
        g_i = rows_ref[8 + q : 9 + q, pl.ds(own, SHARE)]
        d_i = rows_ref[16:17, pl.ds(own, SHARE)]

        def partners(jb, sums, q=q, e_i=e_i, g_i=g_i, d_i=d_i):
            grad_sum, hess_sum = sums
            at = pl.ds(pl.multiple_of(jb * STRETCH, STRETCH), STRETCH)
            e_j = cols_ref[at, q : q + 1]
            g_j = cols_ref[at, 8 + q : 9 + q]
            d_j = cols_ref[at, 16:17]
            inverse = 1.0 / (e_i + e_j)
            gain_gap = g_i - g_j
            higher = gain_gap > 0.0
            part = gain_gap * (jnp.abs(d_i - d_j) * inverse)
            grad = part * jnp.where(higher, e_j, e_i)
            hess = jnp.abs(grad) * (inverse * jnp.where(higher, e_i, e_j))
            grad_sum = grad_sum + jnp.sum(grad.reshape(STRETCH // 32, 32, SHARE), axis=0)
            hess_sum = hess_sum + jnp.sum(hess.reshape(STRETCH // 32, 32, SHARE), axis=0)
            return grad_sum, hess_sum

        zero = jnp.zeros((32, SHARE), jnp.float32)
        last = jnp.where(own < count, (count + STRETCH - 1) // STRETCH, 0)
        grad_sum, hess_sum = lax.fori_loop(0, last, partners, (zero, zero))
        sums_ref[q : q + 1, :] = -jnp.sum(grad_sum, axis=0, keepdims=True)
        sums_ref[8 + q : 9 + q, :] = jnp.sum(hess_sum, axis=0, keepdims=True)

    mine = own + lax.broadcasted_iota(jnp.int32, (query_dev, SHARE), 1) < counts[:query_dev]
    sums_ref[0:query_dev, :] = jnp.where(mine, sums_ref[0:query_dev, :] * inv_ideal, 0.0)
    sums_ref[8 : 8 + query_dev, :] = jnp.where(mine, sums_ref[8 : 8 + query_dev, :] * inv_ideal, 0.0)
    lam_ref[...] = jnp.broadcast_to(sums_ref[...].astype(jnp.bfloat16)[None], lam_ref.shape)


def lambdas(scores, labels, counts):
    query_dev, slots = scores.shape
    vmem = pl.BlockSpec(memory_space=pltpu.VMEM)
    smem = pl.BlockSpec(memory_space=pltpu.SMEM)
    return pl.pallas_call(
        lambda_kernel,
        out_shape=jax.ShapeDtypeStruct((slots // SHARE, 16, SHARE), jnp.bfloat16),
        in_specs=[smem, vmem, vmem],
        out_specs=vmem,
        scratch_shapes=[
            pltpu.VMEM((24, slots), jnp.float32),
            pltpu.VMEM((slots, 24), jnp.float32),
            pltpu.VMEM((16, SHARE), jnp.float32),
        ],
        name="lambdas",
    )(counts, scores, labels)


def prefix_lanes(values):
    lane = lax.broadcasted_iota(jnp.int32, values.shape, 1)
    step = 1
    while step < values.shape[1]:
        values = values + jnp.where(lane >= step, pltpu.roll(values, step, 1), 0.0)
        step *= 2
    return values


def compact(
    smaller_ref, counts_ref, lam_ref, child_ref, codes_ref,
    high_ref, low_ref, weight_ref, moved_ref, spot_ref, chunks_ref,
):
    query_dev, feats, slots = codes_ref.shape
    parents = smaller_ref.shape[0]
    per_group = parents // GROUPS
    blocks = slots // BLOCK
    lam = jnp.concatenate([lam_ref[k].astype(jnp.float32) for k in range(lam_ref.shape[0])], axis=1)
    child = child_ref[...]
    parent = child >> 1
    wanted = jnp.zeros_like(child)
    for p in range(parents):
        wanted = jnp.where(parent == p, smaller_ref[p], wanted)
    position = lax.broadcasted_iota(jnp.int32, child.shape, 1)
    usable = position < count_column(counts_ref)[:query_dev]
    live = ((child & 1) == wanted) & usable
    owner = jnp.where(live, parent // per_group, -1)
    numbers = {}
    ranks = []
    for g in range(0, GROUPS, 2):
        pair = jnp.where(owner == g, 1, jnp.where(owner == g + 1, 4096, 0)).astype(jnp.float32)
        for q in range(query_dev):
            for k in range(blocks):
                total = jnp.sum(pair[q : q + 1, k * BLOCK : (k + 1) * BLOCK]).astype(jnp.int32)
                numbers[g, q, k] = total & 4095
                numbers[g + 1, q, k] = total >> 12
        packed = (prefix_lanes(pair) - pair).astype(jnp.int32)
        ranks += [(packed & 4095).astype(jnp.float32), (packed >> 12).astype(jnp.float32)]
    starts = {}
    base = jnp.int32(0)
    crowded = jnp.int32(0)
    which = lax.broadcasted_iota(jnp.int32, (8, 1), 0)
    for g in range(GROUPS):
        first = base
        opening = jnp.zeros((8, 1), jnp.float32)
        for q in range(query_dev):
            opening = jnp.where(which == q, first.astype(jnp.float32), opening)
            for k in range(blocks):
                starts[g, q, k] = first
                first = first + numbers[g, q, k]
                crowded = jnp.maximum(crowded, numbers[g, q, k])
        spot_ref[g, 0:query_dev, :] = jnp.where(owner == g, ranks[g] + opening[:query_dev], -1.0)
        chunks = (first - base + CHUNK - 1) // CHUNK
        chunks_ref[g, 0] = base // CHUNK
        chunks_ref[g, 1] = chunks
        base = base + chunks * CHUNK

    def clear(t, carry):
        at = pl.ds(pl.multiple_of(t * CHUNK, CHUNK), CHUNK)
        low_ref[:, at] = jnp.zeros((feats, CHUNK), jnp.float32)
        weight_ref[:, at] = jnp.zeros((16, CHUNK), jnp.float32)
        return carry

    lax.fori_loop(0, base // CHUNK, clear, 0)
    local = lax.broadcasted_iota(jnp.int32, (per_group, 1), 0)
    for q in range(query_dev):
        member = ((parent[q : q + 1] % per_group) == local) & live[q : q + 1]
        grad = jnp.where(member, lam[q : q + 1], 0.0)
        hess = jnp.where(member, lam[8 + q : 9 + q], 0.0)
        rows = jnp.concatenate((grad, hess) * GROUPS, axis=0)
        moved_ref[q, 0:feats, :] = codes_ref[q].astype(jnp.float32).astype(jnp.bfloat16)
        moved_ref[q, feats : feats + 16, :] = rows.astype(jnp.bfloat16)
    mark = lax.broadcasted_iota(jnp.int32, (128, 1), 0).astype(jnp.float32)
    lane = lax.broadcasted_iota(jnp.int32, (1, 128), 1)
    one = jnp.ones((), jnp.bfloat16)
    zero = jnp.zeros((), jnp.bfloat16)

    def place(skip):
        for q in range(query_dev):
            for k in range(blocks):
                block = slice(k * BLOCK, (k + 1) * BLOCK)
                moved = moved_ref[q, :, block]
                for g in range(GROUPS):
                    begin = starts[g, q, k]
                    to = pl.multiple_of((begin // 128) * 128, 128)
                    offset = begin - to
                    ahead = spot_ref[g, q : q + 1, block] - (to + skip).astype(jnp.float32)
                    shift = offset.astype(jnp.float32)
                    here = jnp.where((ahead >= shift) & (ahead < shift + 128.0), ahead, -1.0)
                    here = jnp.where(here >= 128.0, here - 128.0, here)
                    hot = jnp.where(here == mark, one, zero)
                    out = lax.dot_general(
                        moved, hot, (((1,), (1,)), ((), ())), preferred_element_type=jnp.float32
                    )
                    now = jnp.where(lane >= offset, out, 0.0)
                    then = jnp.where(lane >= offset, 0.0, out)
                    for add, start in ((now, to + skip), (then, to + skip + 128)):
                        at = pl.ds(pl.multiple_of(start, 128), 128)
                        low_ref[:, at] += add[:feats]
                        weight_ref[:, at] += add[feats:]

    def turn(t, carry):
        place(t * 128)
        return carry

    lax.fori_loop(0, (crowded + 127) // 128, turn, 0)

    def split(t, carry):
        at = pl.ds(pl.multiple_of(t * CHUNK, CHUNK), CHUNK)
        code = low_ref[:, at]
        high = jnp.floor(code * (1.0 / LOWS))
        high_ref[:, at] = high
        low_ref[:, at] = code - high * LOWS
        return carry

    lax.fori_loop(0, base // CHUNK, split, 0)


def histogram_kernel(
    smaller_ref, counts_ref, lam_ref, child_ref, codes_ref, hist_ref,
    high_ref, low_ref, weight_ref, moved_ref, spot_ref, acc_ref, chunks_ref,
):
    feats = hist_ref.shape[0]
    compact(
        smaller_ref, counts_ref, lam_ref, child_ref, codes_ref,
        high_ref, low_ref, weight_ref, moved_ref, spot_ref, chunks_ref,
    )
    kinds = 16 // GROUPS
    wide = HIGHS * kinds
    one = jnp.ones((), jnp.bfloat16)
    zero = jnp.zeros((), jnp.bfloat16)
    low_mark = lax.broadcasted_iota(jnp.int32, (LOWS, 1), 0).astype(jnp.float32).astype(jnp.bfloat16)
    slot = lax.broadcasted_iota(jnp.int32, (16, 1), 0) // kinds
    lane = lax.broadcasted_iota(jnp.int32, (1, 128), 1)
    acc_ref[...] = jnp.zeros_like(acc_ref)
    for g in range(GROUPS):

        def chunk(t, carry, g=g, size=CHUNK):
            at = pl.ds(pl.multiple_of((chunks_ref[g, 0] + t) * CHUNK, CHUNK), size)
            weight = weight_ref[:, at].astype(jnp.bfloat16)
            for first in range(0, feats, HIGHS):
                lhs = []
                rhs = [None] * HIGHS
                for k in range(HIGHS):
                    f = first + k
                    high = jnp.broadcast_to(high_ref[f : f + 1, at], (16, size)).astype(jnp.bfloat16)
                    low = jnp.broadcast_to(low_ref[f : f + 1, at], (LOWS, size)).astype(jnp.bfloat16)
                    for j in range(wide // 16):
                        marks = (slot + j * GROUPS).astype(jnp.float32).astype(jnp.bfloat16)
                        lhs.append(jnp.where(high == marks, weight, zero))
                    rhs[k // GROUPS * GROUPS + (k + g) % GROUPS] = jnp.where(low == low_mark, one, zero)
                out = lax.dot_general(
                    jnp.concatenate(lhs, axis=0), jnp.concatenate(rhs, axis=0),
                    (((1,), (1,)), ((), ())), preferred_element_type=jnp.float32,
                )
                for k in range(HIGHS):
                    half = k // GROUPS * 128
                    mine = lane // LOWS == (k + g) % GROUPS
                    acc_ref[first + k] += jnp.where(
                        mine, out[k * wide : (k + 1) * wide, half : half + 128], 0.0
                    )
            return carry

        def double(t, carry, chunk=chunk):
            return chunk(2 * t, carry, size=2 * CHUNK)

        pairs = chunks_ref[g, 1] // 2
        lax.fori_loop(0, pairs, double, 0)
        lax.fori_loop(2 * pairs, chunks_ref[g, 1], chunk, 0)
    hist_ref[...] = acc_ref[...].astype(jnp.bfloat16)


def histograms(smaller, counts, lam, row_child, bin_codes):
    query_dev, feat_dev, slots = bin_codes.shape
    room = query_dev * slots + GROUPS * CHUNK + BLOCK + 256
    vmem = pl.BlockSpec(memory_space=pltpu.VMEM)
    smem = pl.BlockSpec(memory_space=pltpu.SMEM)
    wide = HIGHS * 16 // GROUPS
    return pl.pallas_call(
        histogram_kernel,
        out_shape=jax.ShapeDtypeStruct((feat_dev, wide, 128), jnp.bfloat16),
        in_specs=[smem, smem, vmem, vmem, vmem],
        out_specs=vmem,
        scratch_shapes=[
            pltpu.VMEM((feat_dev, room), jnp.float32),
            pltpu.VMEM((feat_dev, room), jnp.float32),
            pltpu.VMEM((16, room), jnp.float32),
            pltpu.VMEM((query_dev, feat_dev + 16, slots), jnp.bfloat16),
            pltpu.VMEM((GROUPS, 8, slots), jnp.float32),
            pltpu.VMEM((feat_dev, wide, 128), jnp.float32),
            pltpu.SMEM((GROUPS, 2), jnp.int32),
        ],
        name="histograms",
    )(smaller, counts, lam, row_child, bin_codes)


def gain_kernel(parts_ref, send_ref):
    wide = HIGHS * 16 // GROUPS
    feats = parts_ref.shape[1] // wide
    bins = HIGHS * LOWS
    kinds = 16 // GROUPS
    summed = jnp.sum(parts_ref[...].astype(jnp.float32), axis=0)
    built = []
    for f in range(feats):
        turn = (lax.axis_index("row") * feats + f) % GROUPS
        block = pltpu.roll(summed[f * wide : (f + 1) * wide], (GROUPS - turn) * LOWS % 128, 1)
        stats = ([], [])
        for g in range(GROUPS):
            pieces = [block[h * kinds : (h + 1) * kinds, g * LOWS : (g + 1) * LOWS] for h in range(HIGHS)]
            both = jnp.concatenate(pieces, axis=1)
            stats[0].append(both[: kinds // 2])
            stats[1].append(both[kinds // 2 :])
        built += stats[0] + stats[1]
    built = jnp.concatenate(built, axis=0)
    rows = built.shape[0]
    below = lax.broadcasted_iota(jnp.int32, (bins, bins), 0)
    upto = lax.broadcasted_iota(jnp.int32, (bins, bins), 1)
    left = jnp.dot(
        built, (below <= upto).astype(jnp.float32),
        precision=lax.Precision.HIGHEST, preferred_element_type=jnp.float32,
    )
    threshold = lax.broadcasted_iota(jnp.int32, (8, bins), 1)
    best = jnp.full((8, 1), -jnp.inf, jnp.float32)
    for f in range(feats):
        grad_left = left[f * 16 : f * 16 + 8]
        hess_left = left[f * 16 + 8 : f * 16 + 16]
        grad_total = grad_left[:, bins - 1 : bins]
        hess_total = hess_left[:, bins - 1 : bins]
        grad_right = grad_total - grad_left
        gain = (
            grad_left * grad_left / (hess_left + reg_lambda)
            + grad_right * grad_right / (hess_total - hess_left + reg_lambda)
            - grad_total * grad_total / (hess_total + reg_lambda)
        )
        gain = jnp.where(threshold < bins - 1, gain, -jnp.inf)
        best = jnp.maximum(best, jnp.max(gain, axis=1, keepdims=True))
    stacked = jnp.concatenate(
        (built, jnp.broadcast_to(best, (8, bins)), jnp.zeros((128 - rows - 8, bins), jnp.float32)), axis=0
    )
    by_bin = stacked.T.reshape(send_ref.shape[0], -1, 128)
    half = send_ref.shape[1]
    send_ref[...] = jnp.concatenate((by_bin[:, :half, :64], by_bin[:, half:, :64]), axis=2)


def children_kernel(smaller_ref, parts_ref, parent_ref, children_ref):
    sources, half, lanes = parts_ref.shape
    bin_span, parents, width = children_ref.shape
    group = width // sources
    column = lax.broadcasted_iota(jnp.int32, (sources, width), 1)
    source = lax.broadcasted_iota(jnp.int32, (sources, width), 0)
    outer = sources // INNER
    sender = (source % outer) * INNER + source // outer
    spread = (column // group == sender).astype(jnp.float32)
    rows = group * parents // 2
    row = lax.broadcasted_iota(jnp.int32, (rows, width), 0)
    col = lax.broadcasted_iota(jnp.int32, (rows, width), 1)
    match = (row // (2 * parents) == (col % group) // 4) & ((row // parents) % 2 == col % 2)
    pick_row = lax.broadcasted_iota(jnp.int32, (width // 2, width), 0)
    pick_col = lax.broadcasted_iota(jnp.int32, (width // 2, width), 1)
    pick = (pick_row == (pick_col // 4) * 2 + pick_col % 2).astype(jnp.float32)
    side = (lax.broadcasted_iota(jnp.int32, (parents, width), 1) // 2) % 2
    chosen = side == node_column(smaller_ref, parents)
    parent = jnp.dot(
        parent_ref[...].reshape(bin_span * parents, width // 2), pick,
        precision=lax.Precision.HIGHEST, preferred_element_type=jnp.float32,
    )
    for b in range(bin_span):
        if b < half:
            wide = lax.dot_general(
                parts_ref[:, b, :], spread, (((0,), (0,)), ((), ())),
                precision=lax.Precision.HIGHEST, preferred_element_type=jnp.float32,
            )
            later = (wide[64 : 64 + rows],) if b == 0 else later + (wide[64 : 64 + rows],)
            kept = jnp.where(match, wide[:rows], 0.0)
        else:
            kept = jnp.where(match, later[b - half], 0.0)
        built = jnp.sum(kept.reshape(rows // parents, parents, width), axis=0)
        children_ref[b] = jnp.where(chosen, built, parent[b * parents : (b + 1) * parents] - built)


def shards(scores, labels, counts, bin_codes, row_child, smaller, parent_hist):
    feat_dev = bin_codes.shape[1]
    bin_span, parents, _ = parent_hist.shape
    row_count = lax.axis_size("row")
    feat_count = lax.axis_size("feat")
    rows = feat_dev // row_count * 2 * parents
    bins = bin_span * row_count
    vmem = pl.BlockSpec(memory_space=pltpu.VMEM)
    smem = pl.BlockSpec(memory_space=pltpu.SMEM)
    lam = lax.all_to_all(lambdas(scores, labels, counts), "feat", 0, 0, tiled=True)
    hist = histograms(smaller, counts, lam, row_child, bin_codes)
    outer = row_count // INNER
    across = [[x * INNER + z for x in range(outer)] for z in range(INNER)]
    along = [[x * INNER + z for z in range(INNER)] for x in range(outer)]
    parts = lax.all_to_all(
        hist.reshape(outer, -1, 128), "row", 0, 0, axis_index_groups=across, tiled=True
    )
    parts = jnp.sum(parts.astype(jnp.float32), axis=0).astype(jnp.bfloat16)
    parts = lax.all_to_all(
        parts.reshape(INNER, -1, 128), "row", 0, 0, axis_index_groups=along, tiled=True
    )
    send = pl.pallas_call(
        gain_kernel,
        out_shape=jax.ShapeDtypeStruct((row_count, bin_span // 2, 128), jnp.float32),
        in_specs=[vmem], out_specs=vmem, name="gains",
    )(parts)
    own = lax.all_to_all(
        send.reshape(outer, INNER, bin_span // 2, 128), "row", 0, 0, axis_index_groups=across, tiled=True
    )
    own = lax.all_to_all(
        jnp.transpose(own, (1, 0, 2, 3)), "row", 0, 0, axis_index_groups=along, tiled=True
    ).reshape(row_count, bin_span // 2, 128)
    best = jnp.broadcast_to(jnp.max(own, axis=0)[None], (feat_count, bin_span // 2, 128))
    best = jnp.max(lax.all_to_all(best, "feat", 0, 0, tiled=True), axis=0)
    children = pl.pallas_call(
        children_kernel,
        out_shape=jax.ShapeDtypeStruct((bin_span, parents, feat_dev * 4), jnp.float32),
        in_specs=[smem, vmem, vmem], out_specs=vmem, name="children",
    )(smaller, own, parent_hist)
    return children, best[0, rows : rows + parents]


def solution(mesh):
    placed = (
        P("row", None), P("row", None), P("row"), P("row", "feat", None),
        P("row", None), P(), P("row", None, "feat"),
    )
    return jax.shard_map(
        shards, mesh=mesh, in_specs=placed, out_specs=(P("row", None, "feat"), P()), check_vma=False
    )
```
